32 devices in a mesh: seq: 8 (over z, x), tp: 4 (over y, core).
Axes of the slice: x: 2, y: 2, z: 4, core: 2. Of those that a mesh axis runs over, the one named last changes fastest.
Arguments:
- query_rows: bfloat16 [1024, 2048], P('seq', 'tp'), may hold values from -64 to 64
- key_rows: bfloat16 [1024, 2048], P('seq', 'tp'), may hold values from -4 to 4
- value_rows: bfloat16 [1024, 2048], P('seq', 'tp'), may hold values from -4 to 4
- residual: bfloat16 [1024, 2048], P('seq', 'tp'), may hold values from -40 to 40
- out_weight: bfloat16 [2048, 2048], P('tp'), may hold values from -0.125 to 0.125
- norm_gain: bfloat16 [2048], P('tp'), may hold values from 0.25 to 1.75
- router_weight: bfloat16 [2048, 8], replicated, may hold values from -4 to 4
- expert_ids: int32 [1024, 4], P('seq'), may hold values from 0 to 7, all different within a row; in each aligned block of 128 rows (0 to 127, 128 to 255, ...) at most 128 rows name the same one
- gate_weight: bfloat16 [8, 2048, 1408], P('seq', None, 'tp'), may hold values from -0.125 to 0.125
- up_weight: bfloat16 [8, 2048, 1408], P('seq', None, 'tp'), may hold values from -0.125 to 0.125
- down_weight: bfloat16 [8, 1408, 2048], P('seq', 'tp'), may hold values from -0.15625 to 0.15625
- shared_gate_weight: bfloat16 [2048, 5632], P('seq', 'tp'), may hold values from -0.125 to 0.125
- shared_up_weight: bfloat16 [2048, 5632], P('seq', 'tp'), may hold values from -0.125 to 0.125
- shared_down_weight: bfloat16 [5632, 2048], P('tp', 'seq'), may hold values from -0.078125 to 0.078125
- shared_gate_vector: bfloat16 [2048], replicated, may hold values from -0.125 to 0.125
- segment_ids: int32 [1024], P('seq'), may hold values from 0 to 15, never falling along the last dimension, each value on 1 to 896 neighbouring positions
- pad_mask: int32 [1024], P('seq'), may hold values 0 or 1
- page_table: int32 [32], P('seq'), may hold values from 0 to 31, as said below
Outputs:
- layer_out: float32 [1024, 2048], P('seq', 'tp')
- kv_cache: bfloat16 [32, 32, 4096], P('seq', None, 'tp')
The draws below stay inside these ranges and needn't reach their ends.
Inputs may be any that keep to these rules, and one draw needn't show every extreme that they name: `segment_ids`: Non-decreasing along the stream; every prompt has 1 to 896 tokens and one has exactly 896. `expert_ids`: A token's 4 experts differ. Within the tokens of one device (aligned blocks of 128 tokens) no expert is chosen more than 128 times, and in every draw some expert is chosen exactly 128 times in some block. `page_table`: every slot is named once; a slot s belongs to device s // 4 of seq. There are 4 distinct numbers c_j, common to all devices, such that page j of device d goes to device (d + c_j) mod 8: one device's pages go to 4 different devices, one page each.
All inputs are finite; a program needn't handle non-finite values. No bound on the sum of `pad_mask` on one device may be relied on, other than what follows from the above.
Results may differ from the reference program's by a relative error of at most 0.004.
Values may be sent and summed in bfloat16 or wider, within the bound.
A program may use at most 128 MiB of HBM per device.

```python
import math
import jax
import jax.numpy as jnp
import numpy as np
from jax import lax

D = 2048
HEADS = 16
HD = 128
FF = 1408
SHARED = 5632
TOPK = 4
TOK_DEV = 128
REACH = 7
SEGMENTS = 16
EXPERTS = 8
CAP = 128
PROMPT_MAX = 896
PAGES_DEV = 4
PAGE = 32
TOKENS = 1024
N_SEQ = 8
N_TP = 4


def attention_pair(key):
    base_key = jax.random.fold_in(key, 11)
    key_draw = jax.random.fold_in(base_key, 1)
    query_draw = jax.random.fold_in(base_key, 2)
    shape_rows = (TOKENS, HEADS * HD)
    keys_made = jnp.clip(jax.random.normal(key_draw, shape_rows, jnp.float32), -4.0, 4.0)
    queries_made = jnp.clip(jax.random.normal(query_draw, shape_rows, jnp.float32), -4.0, 4.0)
    return (queries_made, keys_made)


def draw_query_rows(key, part):
    return attention_pair(key)[0].astype(jnp.bfloat16)


def draw_key_rows(key, part):
    return attention_pair(key)[1].astype(jnp.bfloat16)


def draw_residual(key, part):
    rough_key = jax.random.fold_in(key, 21)
    row_key = jax.random.fold_in(key, 22)
    value_key = jax.random.fold_in(key, 23)
    column = jnp.arange(D, dtype=jnp.float32) / (D - 1)
    rough = jnp.exp(jax.random.uniform(rough_key, (D,), jnp.float32, -0.25, 0.25))
    row_scale = jnp.exp(jax.random.uniform(row_key, (TOKENS, 1), jnp.float32, jnp.log(0.5), jnp.log(2.0)))
    ramp = jnp.exp(jnp.log(0.3) + column * (jnp.log(3.0) - jnp.log(0.3)))
    values_made = jnp.clip(jax.random.normal(value_key, (TOKENS, D), jnp.float32), -4.0, 4.0)
    made = values_made * ramp[None, :] * rough[None, :] * row_scale
    return made.astype(jnp.bfloat16)


def draw_router_weight(key, part):
    weight_key = jax.random.fold_in(key, 41)
    made = jnp.clip(jax.random.normal(weight_key, (D, EXPERTS), jnp.float32) * (1.5 / D ** 0.5), -4.0, 4.0)
    return made.astype(jnp.bfloat16)


def draw_page_table(key, part):
    shift_key = jax.random.fold_in(key, 31)
    order_key = jax.random.fold_in(key, 37)
    offsets = jax.random.permutation(shift_key, N_SEQ)[:PAGES_DEV].astype(jnp.int32)
    source = jnp.arange(N_SEQ, dtype=jnp.int32)[:, None]
    owner_dev = (source + offsets[None, :]) % N_SEQ
    orders = jax.vmap(lambda single: jax.random.permutation(single, PAGES_DEV))(jax.random.split(order_key, N_SEQ)).astype(jnp.int32)
    local_slot = orders[owner_dev, jnp.arange(PAGES_DEV, dtype=jnp.int32)[None, :]]
    return (owner_dev * PAGES_DEV + local_slot).reshape(-1).astype(jnp.int32)


def place_ends(drawn, own_key, least, top_value):
    extent = drawn.shape
    index_at = [jax.random.randint(jax.random.fold_in(own_key, axis), (), 0, extent[axis]) for axis in range(len(extent))]
    drawn = drawn.at[tuple(index_at)].set(least)
    longest = extent.index(max(extent))
    index_at[longest] = (index_at[longest] + 1) % extent[longest]
    return drawn.at[tuple(index_at)].set(top_value)


def shard_levels(stream_key, extent, cuts, least, largest):
    loudness = 1.0
    for axis_at, parts in cuts:
        heights = jax.random.uniform(jax.random.fold_in(jax.random.fold_in(stream_key, 6), axis_at), (parts,), jnp.float32, least / len(cuts), largest / len(cuts))
        loudness = loudness * jnp.repeat(jnp.exp(heights), extent[axis_at] // parts).reshape((-1,) + (1,) * (len(extent) - 1 - axis_at))
    return loudness


def split_up(number_of, total, limit, slope):
    loads = [(1 << 20) // math.isqrt(rank ** slope) + 1 for rank in range(2, number_of + 1)]
    surplus, holding = total - limit - (number_of - 1), [1] * (number_of - 1)
    while surplus > 0:
        movable = [i for i in range(number_of - 1) if holding[i] < limit]
        pool, remaining = sum([loads[i] for i in movable]), surplus
        for i in movable:
            extra = min(limit - holding[i], max(1, remaining * loads[i] // pool), surplus)
            holding[i] = holding[i] + extra
            surplus = surplus - extra
    return np.array([limit] + holding)


def ragged_sizes(own_key, count, total, limit, lean):
    if count == 2:
        one = jax.random.randint(own_key, (), max(1, total - limit), min(limit, total - 1) + 1)
        return jnp.stack([one, total - one])
    tallies = jnp.asarray(split_up(count, total, limit, lean), jnp.int32)
    couples = (count - 1) // 2
    giver, receiver = tallies[1:1 + 2 * couples:2], tallies[2:2 + 2 * couples:2]
    room = jnp.minimum(giver - 1, limit - receiver)
    passed = jax.random.randint(jax.random.fold_in(own_key, 1), (couples,), 0, 1 << 20) % (room + 1)
    tallies = tallies.at[1:1 + 2 * couples:2].set(giver - passed).at[2:2 + 2 * couples:2].set(receiver + passed)
    return tallies[jax.random.permutation(jax.random.fold_in(own_key, 2), count)]


def deal_out(key, own, number, rows, count, top, bound, slope):
    order = jax.random.permutation(key, count)
    crowded, usual = shares(count, rows * top, bound, slope, True), shares(count, rows * top, bound, slope, False)
    places = jnp.arange(count)

    def named(lengths, rotation):
        used = int((lengths > 0).sum())
        fixed = max(1, used // 4)
        moved = fixed + (places - fixed + rotation * (used - fixed)) % max(1, count - fixed)
        return jnp.zeros((count,), jnp.int32).at[order[jnp.where(places < fixed, places, moved)]].set(jnp.asarray(lengths, jnp.int32))

    lengths = jnp.where(number % 4 == 0, named(crowded, number // 4), named(usual, number - number // 4 - 1))
    mixed = jax.random.permutation(jax.random.fold_in(own, 3), count)
    giver, sink = mixed[0:count // 2 * 2:2], mixed[1:count // 2 * 2:2]
    room = jnp.minimum(lengths[giver] - 1, bound - lengths[sink]) // 2
    room = jnp.where((giver == order[0]) | (sink == order[0]) | (lengths[sink] == 0), 0, jnp.maximum(room, 0))
    moved = jax.random.randint(jax.random.fold_in(own, 4), (count // 2,), 0, 1 << 20) % (room + 1)
    lengths = lengths.at[giver].add(-moved).at[sink].add(moved)
    items = jnp.searchsorted(jnp.cumsum(lengths), jnp.arange(rows * top), side="right").astype(jnp.int32)
    table = items.reshape(top, rows).T
    table = table[jax.random.permutation(jax.random.fold_in(own, 1), rows)]
    rotation = jax.random.randint(jax.random.fold_in(own, 2), (rows, 1), 0, top)
    return jnp.take_along_axis(table, (jnp.arange(top)[None, :] + rotation) % top, axis=1)


def shares(number_of, total, bound, lean, full):
    portions = [(1 << 20) // math.isqrt(grade ** lean) + 1 for grade in range(1, number_of + 1)]
    largest = bound if full else min(bound, max(-(-total // number_of), total * portions[0] // sum(portions)))
    least = 1 if total - largest >= number_of - 1 else 0
    counts, spare = [largest] + [least] * (number_of - 1), total - largest - least * (number_of - 1)
    while spare > 0:
        free = [i for i in range(1, number_of) if counts[i] < largest] or [i for i in range(1, number_of) if counts[i] < bound]
        whole, left = sum([portions[i] for i in free]), spare
        for i in free:
            more = min(bound - counts[i], max(1, left * portions[i] // whole), spare)
            counts[i] = counts[i] + more
            spare = spare - more
    return np.array(counts)


def centred(key, shape, deviation, limit, cuts=(), kind=jnp.bfloat16):
    drawn = jax.random.normal(key, shape, jnp.float32) * deviation
    if len(cuts) > 0:
        drawn = shard_levels(key, shape, cuts, -0.22, 0.18) * drawn
    return jnp.clip(drawn, min=-limit, max=limit).astype(kind)


def setup_inputs(seed: int = 0) -> dict:
    seeds = jax.random.split(jax.random.key(seed), 19)
    query_rows = draw_query_rows(jax.random.fold_in(seeds[18], 71), 0)
    key_rows = draw_key_rows(jax.random.fold_in(seeds[18], 71), 0)
    value_rows = centred(seeds[2], (TOKENS, HEADS * HD), 1.0, 4.0, ((0, 8), (1, 4)))
    residual = draw_residual(jax.random.fold_in(seeds[18], 71), 0)
    out_weight = centred(seeds[4], (HEADS * HD, D), (HEADS * HD) ** -0.5, 0.125, ((0, 4),))
    norm_gain = jnp.clip(1.0 + 0.15 * jax.random.normal(seeds[5], (D,), jnp.float32), 0.25, 1.75).astype(jnp.bfloat16)
    router_weight = draw_router_weight(jax.random.fold_in(seeds[18], 71), 0)
    expert_ids_keys = jax.random.split(jax.random.fold_in(seeds[7], 1), TOKENS // TOK_DEV)
    expert_ids_turns = jax.random.permutation(jax.random.fold_in(seeds[7], 3), TOKENS // TOK_DEV)
    expert_ids = jax.vmap(lambda own, number: deal_out(jax.random.fold_in(seeds[7], 2), own, number, TOK_DEV, EXPERTS, TOPK, CAP, 1))(expert_ids_keys, expert_ids_turns).reshape((TOKENS, TOPK))
    gate_weight = centred(seeds[8], (EXPERTS, D, FF), D ** -0.5, 0.125, ((0, 8), (2, 4)))
    up_weight = centred(seeds[9], (EXPERTS, D, FF), D ** -0.5, 0.125, ((0, 8), (2, 4)))
    down_weight = centred(seeds[10], (EXPERTS, FF, D), FF ** -0.5, 0.15625, ((0, 8), (1, 4)))
    shared_gate_weight = centred(seeds[11], (D, SHARED), D ** -0.5, 0.125, ((0, 8), (1, 4)))
    shared_up_weight = centred(seeds[12], (D, SHARED), D ** -0.5, 0.125, ((0, 8), (1, 4)))
    shared_down_weight = centred(seeds[13], (SHARED, D), SHARED ** -0.5, 0.078125, ((0, 4), (1, 8)))
    shared_gate_vector = centred(seeds[14], (D,), D ** -0.5, 0.125)
    segment_ids = jnp.searchsorted(jnp.cumsum(ragged_sizes(seeds[15], SEGMENTS, TOKENS, PROMPT_MAX, 1)), jnp.arange(TOKENS), side="right").astype(jnp.int32)
    pad_mask = place_ends((jax.random.randint(seeds[16], (TOKENS,), 0, 8) < 7).astype(jnp.int32), jax.random.fold_in(seeds[16], 1), 0, 1)
    page_table = draw_page_table(jax.random.fold_in(seeds[18], 71), 0)
    return {"query_rows": query_rows, "key_rows": key_rows, "value_rows": value_rows, "residual": residual, "out_weight": out_weight, "norm_gain": norm_gain, "router_weight": router_weight, "expert_ids": expert_ids, "gate_weight": gate_weight, "up_weight": up_weight, "down_weight": down_weight, "shared_gate_weight": shared_gate_weight, "shared_up_weight": shared_up_weight, "shared_down_weight": shared_down_weight, "shared_gate_vector": shared_gate_vector, "segment_ids": segment_ids, "pad_mask": pad_mask, "page_table": page_table}


norm_eps = 1e-06

def reference(query_rows, key_rows, value_rows, residual, out_weight, norm_gain, router_weight, expert_ids, gate_weight, up_weight, down_weight, shared_gate_weight, shared_up_weight, shared_down_weight, shared_gate_vector, segment_ids, pad_mask, page_table):
    front = REACH * TOK_DEV
    span = front + TOK_DEV
    feat_width = HEADS * HD
    pad_keys = jnp.concatenate([jnp.zeros((front, feat_width), jnp.bfloat16), key_rows], 0)
    pad_values = jnp.concatenate([jnp.zeros((front, feat_width), jnp.bfloat16), value_rows], 0)
    pad_segment = jnp.concatenate([jnp.full((front,), -1, jnp.int32), segment_ids], 0)
    pad_live = jnp.concatenate([jnp.zeros((front,), jnp.int32), pad_mask], 0)
    score_scale = HD ** (-0.5)

    def attend(block_index):
        start = (block_index * TOK_DEV).astype(jnp.int32)
        query_heads = lax.dynamic_slice_in_dim(query_rows, start, TOK_DEV, 0).astype(jnp.float32).reshape(TOK_DEV, HEADS, HD)
        key_heads = lax.dynamic_slice_in_dim(pad_keys, start, span, 0).astype(jnp.float32).reshape(span, HEADS, HD)
        value_heads = lax.dynamic_slice_in_dim(pad_values, start, span, 0).astype(jnp.float32).reshape(span, HEADS, HD)
        query_seg = lax.dynamic_slice_in_dim(segment_ids, start, TOK_DEV, 0)
        key_seg = lax.dynamic_slice_in_dim(pad_segment, start, span, 0)
        key_live = lax.dynamic_slice_in_dim(pad_live, start, span, 0)
        query_pos = start + jnp.arange(TOK_DEV, dtype=jnp.int32)
        key_pos = start - front + jnp.arange(span, dtype=jnp.int32)
        same_place = key_pos[None, :] == query_pos[:, None]
        visible = (query_seg[:, None] == key_seg[None, :]) & (key_pos[None, :] <= query_pos[:, None]) & ((key_live[None, :] == 1) | same_place)
        scores = jnp.einsum('qhd,khd->hqk', query_heads, key_heads) * score_scale
        scores = jnp.where(visible[None], scores, -jnp.inf)
        row_top = lax.optimization_barrier(jnp.max(scores, -1))
        weights_raw = jnp.exp(scores - row_top[..., None])
        row_total = lax.optimization_barrier(jnp.sum(weights_raw, -1))
        weights_low = lax.optimization_barrier(weights_raw.astype(jnp.bfloat16)).astype(jnp.float32)
        mixed_heads = jnp.einsum('hqk,khd->qhd', weights_low, value_heads)
        return (mixed_heads / row_total.T[:, :, None]).astype(jnp.bfloat16).reshape(TOK_DEV, feat_width)
    attended = lax.map(attend, jnp.arange(N_SEQ, dtype=jnp.int32)).reshape(TOKENS, feat_width)
    stream = residual.astype(jnp.float32) + jnp.dot(attended, out_weight, preferred_element_type=jnp.float32)
    square_sum = lax.optimization_barrier(jnp.sum(stream * stream, 1))
    normed = (stream * lax.rsqrt(square_sum / D + norm_eps)[:, None] * norm_gain.astype(jnp.float32)).astype(jnp.bfloat16)
    logits = jnp.dot(normed, router_weight, preferred_element_type=jnp.float32)
    chosen_logits = jnp.take_along_axis(logits, expert_ids, 1)
    choice_top = lax.optimization_barrier(jnp.max(chosen_logits, 1, keepdims=True))
    choice_exp = jnp.exp(chosen_logits - choice_top)
    route_weight = choice_exp / lax.optimization_barrier(jnp.sum(choice_exp, 1, keepdims=True))
    expert_match = expert_ids[:, :, None] == jnp.arange(EXPERTS, dtype=jnp.int32)[None, None, :]
    weight_table = lax.optimization_barrier(jnp.sum(jnp.where(expert_match, route_weight[:, :, None], jnp.float32(0.0)), 1))
    picks = TOK_DEV * TOPK
    flat_expert = expert_ids.reshape(N_SEQ, picks)
    onehot = (flat_expert[:, :, None] == jnp.arange(EXPERTS, dtype=jnp.int32)[None, None, :]).astype(jnp.int32)
    slot_rank = (lax.optimization_barrier(jnp.sum(jnp.cumsum(onehot, 1) * onehot, 2)) - 1).astype(jnp.int32)
    source_index = jnp.broadcast_to(jnp.arange(N_SEQ, dtype=jnp.int32)[:, None], (N_SEQ, picks))
    token_index = (source_index * TOK_DEV + jnp.arange(picks, dtype=jnp.int32)[None, :] // TOPK).astype(jnp.int32)
    table = jnp.full((N_SEQ, EXPERTS, CAP), TOKENS, jnp.int32).at[source_index, flat_expert, slot_rank].set(token_index)
    ff_group = FF // N_TP
    normed_pad = jnp.concatenate([normed, jnp.zeros((1, D), jnp.bfloat16)], 0)
    probs_pad = jnp.concatenate([weight_table, jnp.zeros((1, EXPERTS), weight_table.dtype)], 0)

    def one_expert(mixture, expert_index):
        token_list = lax.dynamic_index_in_dim(table, expert_index, 1, False).reshape(-1)
        rows_in = normed_pad[token_list]
        w_gate = lax.dynamic_index_in_dim(gate_weight, expert_index, 0, False)
        w_up = lax.dynamic_index_in_dim(up_weight, expert_index, 0, False)
        w_down = lax.dynamic_index_in_dim(down_weight, expert_index, 0, False)
        gate_act = jnp.dot(rows_in, w_gate, preferred_element_type=jnp.float32)
        up_act = jnp.dot(rows_in, w_up, preferred_element_type=jnp.float32)
        hidden = (jax.nn.silu(gate_act) * up_act).astype(jnp.bfloat16)
        summed = jnp.zeros((rows_in.shape[0], D), jnp.float32)
        for group_index in range(N_TP):
            group_part = jnp.dot(hidden[:, group_index * ff_group:(group_index + 1) * ff_group], w_down[group_index * ff_group:(group_index + 1) * ff_group], preferred_element_type=jnp.float32)
            summed = summed + lax.optimization_barrier(group_part.astype(jnp.bfloat16)).astype(jnp.float32)
        expert_out = lax.optimization_barrier(summed.astype(jnp.bfloat16)).astype(jnp.float32)
        gate_col = lax.dynamic_index_in_dim(probs_pad, expert_index, 1, False)[token_list]
        return (mixture.at[token_list].add(expert_out * gate_col[:, None], mode='drop'), None)
    mixture, unused = lax.scan(one_expert, jnp.zeros((TOKENS, D), jnp.float32), jnp.arange(EXPERTS, dtype=jnp.int32))

    def shared_block(block_index):
        start = (block_index * TOK_DEV).astype(jnp.int32)
        rows_in = lax.dynamic_slice_in_dim(normed, start, TOK_DEV, 0)
        shared_gate_act = jnp.dot(rows_in, shared_gate_weight, preferred_element_type=jnp.float32)
        shared_up_act = jnp.dot(rows_in, shared_up_weight, preferred_element_type=jnp.float32)
        shared_hidden = (jax.nn.silu(shared_gate_act) * shared_up_act).astype(jnp.bfloat16)
        shared_out = jnp.dot(shared_hidden, shared_down_weight, preferred_element_type=jnp.float32)
        shared_scale = jax.nn.sigmoid(jnp.dot(rows_in, shared_gate_vector, preferred_element_type=jnp.float32))
        return shared_out * shared_scale[:, None]
    shared_term = lax.map(shared_block, jnp.arange(N_SEQ, dtype=jnp.int32)).reshape(TOKENS, D)
    layer_out = stream + mixture + shared_term
    stretch_width = HEADS * HD // N_TP
    kv_rows = jnp.stack([key_rows.reshape(TOKENS, N_TP, stretch_width), value_rows.reshape(TOKENS, N_TP, stretch_width)], 2)
    kv_pages = kv_rows.reshape(TOKENS // PAGE, PAGE, 2 * HEADS * HD)
    kv_cache = jnp.zeros_like(kv_pages).at[page_table].set(kv_pages)
    return (layer_out, kv_cache)
```

```python
import functools

import jax
import jax.numpy as jnp
from jax import lax
from jax.experimental import pallas as pl
from jax.experimental.pallas import tpu as pltpu
from jax.sharding import PartitionSpec as P

D = 2048
HD = 128
REACH = 7


norm_eps = 1e-06


MESH = pl.DeviceIdType.MESH
BF16, F32 = jnp.bfloat16, jnp.float32


def place(seq_count):
    me, tp = lax.axis_index("seq"), lax.axis_index("tp")
    return me, tp, me // 2, lax.rem(me, 2), seq_count // 2


def greet(peers):
    barrier = pltpu.get_barrier_semaphore()
    for peer in peers:
        pl.semaphore_signal(barrier, inc=1, device_id=peer, device_id_type=MESH)
    pl.semaphore_wait(barrier, len(peers))


def remote(src, dst, sems, index, peer):
    copy = pltpu.make_async_remote_copy(
        src_ref=src,
        dst_ref=dst,
        send_sem=sems[0].at[index],
        recv_sem=sems[1].at[index],
        device_id=peer,
        device_id_type=MESH,
    )
    copy.start()
    return copy


def swap_rows(source, target, sems, first, others, me, tp):
    depth = source.shape[1]
    rows = pl.ds(pl.multiple_of(me * depth, depth), depth)
    return [
        remote(source.at[other], target.at[rows, :], sems, first + index, (other, tp))
        for index, other in enumerate(others)
    ]


def gather_kernel(
    seq_count,
    kv_ref,
    notes_ref,
    gate_ref,
    up_ref,
    down_ref,
    all_kv,
    all_notes,
    gate_split,
    up_split,
    down_full,
    send,
    recv,
    local,
):
    me, tp, z, x, groups = place(seq_count)
    tokens = kv_ref.shape[0]
    sems = (send, recv)
    pair = (z * 2 + 1 - x, tp)
    column = [(lax.rem(z + k, groups) * 2 + x, tp) for k in range(1, groups)]
    others = [lax.rem(me + k, seq_count) for k in range(1, seq_count)]
    greet([(other, tp) for other in others])
    units, depth = down_full.shape[0], down_ref.shape[1]

    def down_rows(owner):
        return down_ref.at[pl.ds(pl.multiple_of(owner * units, units), units), :]

    down_view = down_full.at[:, pl.ds(pl.multiple_of(me * depth, depth), depth)]

    def views(owner):
        row = pl.multiple_of(owner * tokens, tokens)
        return all_notes.at[owner], all_kv.at[pl.ds(row, tokens), :]

    sources = (notes_ref, kv_ref)
    keep = [
        pltpu.make_async_copy(source, view, local.at[index])
        for index, (source, view) in enumerate(zip(sources, views(me)))
    ]
    keep.append(pltpu.make_async_copy(down_rows(me), down_view, local.at[2]))
    for copy in keep:
        copy.start()
    steps = 2 * groups - 1
    down, across = [], []
    for kind in range(2):
        for k in range(1, groups):
            down.append(
                remote(sources[kind], views(me)[kind], sems, kind * steps + k - 1, column[k - 1])
            )
        across.append(
            remote(sources[kind], views(me)[kind], sems, kind * steps + groups - 1, pair)
        )
    swapped = [
        remote(down_rows(other), down_view, sems, 2 * steps + index, (other, tp))
        for index, other in enumerate(others)
    ]
    for source, split in ((gate_ref, gate_split), (up_ref, up_split)):
        for owner in range(seq_count):
            split[owner] = source[:, owner * units : (owner + 1) * units]
    for kind in range(2):
        for k in range(1, groups):
            down[kind * (groups - 1) + k - 1].wait_recv()
            view = views(lax.rem(z + groups - k, groups) * 2 + x)[kind]
            across.append(remote(view, view, sems, kind * steps + groups - 1 + k, pair))
    for copy in across + swapped:
        copy.wait_recv()
    for copy in down + across + swapped:
        copy.wait_send()
    for copy in keep:
        copy.wait()


def gather_over_seq(kv_local, notes, shared_gate_weight, shared_up_weight, shared_down_weight):
    seq_count = lax.axis_size("seq")
    tokens, width = kv_local.shape
    count = 3 * (seq_count - 1)
    depth, hidden = shared_gate_weight.shape
    units = hidden // seq_count
    split = jax.ShapeDtypeStruct((seq_count, depth, units), BF16)
    return pl.pallas_call(
        functools.partial(gather_kernel, seq_count),
        out_shape=(
            jax.ShapeDtypeStruct((seq_count * tokens, width), BF16),
            jax.ShapeDtypeStruct((seq_count,) + notes.shape, jnp.int32),
            split,
            split,
            jax.ShapeDtypeStruct((units, depth * seq_count), BF16),
        ),
        in_specs=[pl.BlockSpec(memory_space=pl.ANY)] * 2
        + [pl.BlockSpec(memory_space=pltpu.VMEM)] * 2
        + [pl.BlockSpec(memory_space=pl.ANY)],
        out_specs=[pl.BlockSpec(memory_space=pl.ANY)] * 2
        + [pl.BlockSpec(memory_space=pltpu.VMEM)] * 2
        + [pl.BlockSpec(memory_space=pl.ANY)],
        scratch_shapes=[
            pltpu.SemaphoreType.DMA((count,)),
            pltpu.SemaphoreType.DMA((count,)),
            pltpu.SemaphoreType.DMA((3,)),
        ],
        compiler_params=pltpu.CompilerParams(
            collective_id=0, has_side_effects=True, vmem_limit_bytes=24 * 2**20
        ),
        cost_estimate=pl.CostEstimate(flops=0, transcendentals=0, bytes_accessed=120_000_000),
    )(kv_local, notes, shared_gate_weight, shared_up_weight, shared_down_weight)


def norm_kernel(
    seq_count,
    attended,
    out_weight,
    residual,
    gain,
    gate_split,
    up_split,
    stream,
    rows,
    gate_full,
    up_full,
    part_out,
    part_in,
    square_out,
    square_in,
    normed,
    tp_send,
    tp_recv,
    send,
    recv,
    swap_send,
    swap_recv,
    local,
):
    me, tp, z, x, groups = place(seq_count)
    tokens, width = residual.shape
    others = [lax.rem(me + k, seq_count) for k in range(1, seq_count)]
    depth = gate_split.shape[1]
    own_depth = pl.ds(pl.multiple_of(me * depth, depth), depth)
    swap_sems = (swap_send, swap_recv)
    tp_sems, sems = (tp_send, tp_recv), (send, recv)
    pair = (z * 2 + 1 - x, tp)
    column = [(lax.rem(z + k, groups) * 2 + x, tp) for k in range(1, groups)]
    row_peers = [(me, lax.rem(tp + k, 4)) for k in range(1, 4)]
    core_tp = (tp // 2) * 2 + 1 - lax.rem(tp, 2)
    far_tp = lax.rem(tp + 2, 4)
    core, far = (me, core_tp), (me, far_tp)
    greet([(other, tp) for other in others] + row_peers)
    swapped = swap_rows(gate_split, gate_full, swap_sems, 0, others, me, tp)
    keep = [
        pltpu.make_async_copy(split.at[me], full.at[own_depth, :], local.at[index])
        for index, (split, full) in enumerate(((gate_split, gate_full), (up_split, up_full)))
    ]

    def part(owner):
        start = pl.multiple_of(owner * width, width)
        return jnp.dot(
            attended[...], out_weight[:, pl.ds(start, width)], preferred_element_type=F32
        )

    copies = []
    for k in (2, 1, 3):
        part_out[k - 1] = part(lax.rem(tp + k, 4)).astype(BF16)
        copies.append(
            remote(part_out.at[k - 1], part_in.at[k - 1], tp_sems, k - 1, row_peers[k - 1])
        )
    total = residual[...].astype(F32) + part(tp)
    for copy in copies:
        copy.wait_recv()
    for k in range(3):
        total += part_in[k].astype(F32)
    stream[...] = total
    squares = total * total
    lanes = squares[:, :128]
    for start in range(128, width, 128):
        lanes += squares[:, start : start + 128]
    square_out[...] = lanes
    square_copies = [
        remote(square_out, square_in.at[k], tp_sems, 3 + k, row_peers[k]) for k in range(3)
    ]
    for copy in square_copies:
        copy.wait_recv()
    lanes = lanes + square_in[0] + square_in[1] + square_in[2]
    square_sum = jnp.sum(lanes, axis=1, keepdims=True)
    normed[...] = (
        total * lax.rsqrt(square_sum / D + norm_eps) * gain[...].astype(F32)
    ).astype(BF16)

    def view(owner, tp_owner):
        row = pl.multiple_of(owner * tokens, tokens)
        col = pl.multiple_of(tp_owner * width, width)
        return rows.at[pl.ds(row, tokens), pl.ds(col, width)]

    mine = view(me, tp)
    keep.append(pltpu.make_async_copy(normed, mine, local.at[2]))
    for copy in keep:
        copy.start()
    first_across, first_far = groups - 1, 2 * groups - 1
    first_core = first_far + seq_count
    down = [remote(normed, mine, sems, k, column[k]) for k in range(groups - 1)]
    across = [remote(normed, mine, sems, first_across, pair)]
    distant = [remote(normed, mine, sems, first_far, far)]
    near = [remote(normed, mine, sems, first_core, core)]
    swapped += swap_rows(up_split, up_full, swap_sems, seq_count - 1, others, me, tp)
    owners = [me]
    for k in range(1, groups):
        down[k - 1].wait_recv()
        owner = lax.rem(z + groups - k, groups) * 2 + x
        owners.append(owner)
        block = view(owner, tp)
        across.append(remote(block, block, sems, first_across + k, pair))
        distant.append(remote(block, block, sems, first_far + k, far))
        near.append(remote(block, block, sems, first_core + k, core))
    for k in range(groups):
        across[k].wait_recv()
        owner = lax.rem(z + groups - k, groups) * 2 + 1 - x
        owners.append(owner)
        block = view(owner, tp)
        distant.append(remote(block, block, sems, first_far + groups + k, far))
        near.append(remote(block, block, sems, first_core + groups + k, core))
    for k in range(seq_count):
        distant[k].wait_recv()
        block = view(owners[k], far_tp)
        near.append(remote(block, block, sems, first_core + seq_count + k, core))
    for copy in near + swapped:
        copy.wait_recv()
    for copy in copies + square_copies + down + across + distant + near + swapped:
        copy.wait_send()
    for copy in keep:
        copy.wait()


def project_and_norm(attended, out_weight, residual, norm_gain, gate_split, up_split):
    seq_count = lax.axis_size("seq")
    tokens, width = residual.shape
    count = 2 * (seq_count // 2) - 1 + 3 * seq_count
    swaps = 2 * (seq_count - 1)
    full = jax.ShapeDtypeStruct((seq_count * gate_split.shape[1], gate_split.shape[2]), BF16)
    return pl.pallas_call(
        functools.partial(norm_kernel, seq_count),
        out_shape=(
            jax.ShapeDtypeStruct((tokens, width), F32),
            jax.ShapeDtypeStruct((seq_count * tokens, 4 * width), BF16),
            full,
            full,
        ),
        in_specs=[pl.BlockSpec(memory_space=pltpu.VMEM)] * 4
        + [pl.BlockSpec(memory_space=pl.ANY)] * 2,
        out_specs=[pl.BlockSpec(memory_space=pltpu.VMEM)]
        + [pl.BlockSpec(memory_space=pl.ANY)] * 3,
        scratch_shapes=[
            pltpu.VMEM((3, tokens, width), BF16),
            pltpu.VMEM((3, tokens, width), BF16),
            pltpu.VMEM((tokens, 128), F32),
            pltpu.VMEM((3, tokens, 128), F32),
            pltpu.VMEM((tokens, width), BF16),
            pltpu.SemaphoreType.DMA((6,)),
            pltpu.SemaphoreType.DMA((6,)),
            pltpu.SemaphoreType.DMA((count,)),
            pltpu.SemaphoreType.DMA((count,)),
            pltpu.SemaphoreType.DMA((swaps,)),
            pltpu.SemaphoreType.DMA((swaps,)),
            pltpu.SemaphoreType.DMA((3,)),
        ],
        compiler_params=pltpu.CompilerParams(
            collective_id=1, has_side_effects=True, vmem_limit_bytes=32 * 2**20
        ),
        cost_estimate=pl.CostEstimate(flops=0, transcendentals=0, bytes_accessed=150_000_000),
    )(attended, out_weight, residual, norm_gain.reshape(1, width), gate_split, up_split)


def reduce_kernel(
    seq_count,
    hidden,
    shared_hidden,
    down_weight,
    shared_down,
    out,
    core_out,
    core_in,
    far_out,
    far_in,
    pair_out,
    pair_in,
    down_out,
    down_in,
    kept,
    half,
    send,
    recv,
):
    me, tp, z, x, groups = place(seq_count)
    tokens, width = out.shape
    y, c = tp // 2, lax.rem(tp, 2)
    sems = (send, recv)
    pair = (z * 2 + 1 - x, tp)
    column = [(lax.rem(z + k, groups) * 2 + x, tp) for k in range(1, groups)]
    core, far = (me, y * 2 + 1 - c), (me, lax.rem(tp + 2, 4))
    greet([pair, core, far] + column)
    first_far, first_pair, first_down = 2 * groups, 3 * groups, 4 * groups

    def cols(tp_owner):
        return pl.ds(pl.multiple_of(tp_owner * width, width), width)

    def chunk(k):
        return pl.ds(pl.multiple_of(lax.rem(z + k, groups) * 2 * tokens, 2 * tokens), 2 * tokens)

    def product(k, tp_owner):
        return jnp.dot(
            hidden[chunk(k), :], down_weight[:, cols(tp_owner)], preferred_element_type=F32
        ) + jnp.dot(
            shared_hidden[chunk(k), :], shared_down[:, cols(tp_owner)], preferred_element_type=F32
        )

    order = list(range(1, groups)) + [0]
    to_core, to_far, to_pair, to_down = {}, {}, {}, []

    def start_core(k):
        to_core[k] = []
        for part in range(2):
            core_out[k, part] = product(k, part * 2 + 1 - c).astype(BF16)
            to_core[k].append(
                remote(core_out.at[k, part], core_in.at[k, part], sems, 2 * k + part, core)
            )

    start_core(order[0])
    for step in range(groups + 2):
        if step + 1 < groups:
            start_core(order[step + 1])
        if step < groups:
            k = order[step]
            sent = product(k, (1 - y) * 2 + c)
            kept[k] = product(k, tp)
            for copy in to_core[k]:
                copy.wait_recv()
            far_out[k] = (sent + core_in[k, 1 - y].astype(F32)).astype(BF16)
            to_far[k] = remote(far_out.at[k], far_in.at[k], sems, first_far + k, far)
            kept[k] = kept[k] + core_in[k, y].astype(F32)
        if 0 <= step - 1 < groups:
            k = order[step - 1]
            to_far[k].wait_recv()
            kept[k] = kept[k] + far_in[k].astype(F32)
            away = pl.ds(pl.multiple_of((1 - x) * tokens, tokens), tokens)
            pair_out[k] = kept[k, away, :].astype(BF16)
            to_pair[k] = remote(pair_out.at[k], pair_in.at[k], sems, first_pair + k, pair)
        if 0 <= step - 2 < groups:
            k = order[step - 2]
            to_pair[k].wait_recv()
            here = pl.ds(pl.multiple_of(x * tokens, tokens), tokens)
            value = kept[k, here, :] + pair_in[k].astype(F32)
            if k == 0:
                half[...] = value
            else:
                down_out[k - 1] = value.astype(BF16)
                to_down.append(
                    remote(
                        down_out.at[k - 1],
                        down_in.at[k - 1],
                        sems,
                        first_down + k - 1,
                        column[k - 1],
                    )
                )
    for copy in to_down:
        copy.wait_recv()
    value = half[...]
    for k in range(groups - 1):
        value += down_in[k].astype(F32)
    out[...] = value
    for k in range(groups):
        for copy in to_core[k] + [to_far[k], to_pair[k]]:
            copy.wait_send()
    for copy in to_down:
        copy.wait_send()


def reduce_all(hidden, shared_hidden, down_weight, shared_down):
    seq_count = lax.axis_size("seq")
    groups = seq_count // 2
    tokens, width = hidden.shape[0] // seq_count, down_weight.shape[1] // 4
    count = 5 * groups - 1
    return pl.pallas_call(
        functools.partial(reduce_kernel, seq_count),
        out_shape=jax.ShapeDtypeStruct((tokens, width), F32),
        in_specs=[pl.BlockSpec(memory_space=pltpu.VMEM)] * 4,
        out_specs=pl.BlockSpec(memory_space=pltpu.VMEM),
        scratch_shapes=[
            pltpu.VMEM((groups, 2, 2 * tokens, width), BF16),
            pltpu.VMEM((groups, 2, 2 * tokens, width), BF16),
            pltpu.VMEM((groups, 2 * tokens, width), BF16),
            pltpu.VMEM((groups, 2 * tokens, width), BF16),
            pltpu.VMEM((groups, tokens, width), BF16),
            pltpu.VMEM((groups, tokens, width), BF16),
            pltpu.VMEM((groups - 1, tokens, width), BF16),
            pltpu.VMEM((groups - 1, tokens, width), BF16),
            pltpu.VMEM((groups, 2 * tokens, width), F32),
            pltpu.VMEM((tokens, width), F32),
            pltpu.SemaphoreType.DMA((count,)),
            pltpu.SemaphoreType.DMA((count,)),
        ],
        compiler_params=pltpu.CompilerParams(
            collective_id=2, has_side_effects=True, vmem_limit_bytes=40 * 2**20
        ),
        cost_estimate=pl.CostEstimate(flops=0, transcendentals=0, bytes_accessed=150_000_000),
    )(hidden, shared_hidden, down_weight, shared_down)


def head_scores(query_heads, key_heads):
    score_scale = query_heads.shape[-1] ** (-0.5)
    return (
        jnp.einsum("qhd,khd->hqk", query_heads, key_heads, preferred_element_type=jnp.float32)
        * score_scale
    )


def run_experts(rows_in, gate_weight, up_weight, down_weight):
    local_experts = gate_weight.shape[0]
    sources = rows_in.shape[0] // local_experts
    grouped = rows_in.reshape(sources, local_experts, rows_in.shape[1], rows_in.shape[2])
    gate_act = jnp.einsum(
        "nesd,edf->nesf", grouped, gate_weight, preferred_element_type=jnp.float32
    )
    up_act = jnp.einsum("nesd,edf->nesf", grouped, up_weight, preferred_element_type=jnp.float32)
    hidden = (jax.nn.silu(gate_act) * up_act).astype(jnp.bfloat16)
    partial_out = jnp.einsum(
        "nesf,efd->nesd", hidden, down_weight, preferred_element_type=jnp.float32
    )
    partial_out = partial_out.reshape(rows_in.shape[0], rows_in.shape[1], down_weight.shape[2])
    summed = lax.psum_scatter(
        partial_out.astype(jnp.bfloat16), "tp", scatter_dimension=2, tiled=True
    )
    return lax.all_to_all(summed, "seq", split_axis=0, concat_axis=0, tiled=True)


def everywhere(
    rows,
    all_notes,
    router_weight,
    shared_gate_vector,
    gate_weight,
    up_weight,
    down_weight,
    shared_gate,
    shared_up,
    shared_down,
    per_token,
):
    me = lax.axis_index("seq")
    tokens_here = rows.shape[0] // lax.axis_size("seq")
    logits = jnp.dot(rows, router_weight, preferred_element_type=jnp.float32)
    ids = all_notes[:, 2 * tokens_here : (2 + per_token) * tokens_here]
    ids = ids.reshape(-1, per_token, tokens_here).transpose(0, 2, 1).reshape(-1, per_token)
    expert_range = jnp.arange(logits.shape[1], dtype=jnp.int32)
    chosen = jnp.any(ids[:, :, None] == expert_range[None, None, :], 1)
    chosen_logits = jnp.where(chosen, logits, -jnp.inf)
    choice_exp = jnp.exp(chosen_logits - jnp.max(chosen_logits, 1, keepdims=True))
    route_weight = choice_exp / jnp.sum(choice_exp, 1, keepdims=True)
    shared_scale = jax.nn.sigmoid(
        jnp.dot(rows, shared_gate_vector, preferred_element_type=jnp.float32)
    )

    def hidden_of(gate, up, scale):
        gate_act = jnp.dot(rows, gate, preferred_element_type=jnp.float32)
        up_act = jnp.dot(rows, up, preferred_element_type=jnp.float32)
        return (jax.nn.silu(gate_act) * up_act * scale[:, None]).astype(jnp.bfloat16)

    scale = jnp.sum(jnp.where(expert_range[None, :] == me, route_weight, 0.0), 1)
    return reduce_all(
        hidden_of(gate_weight[0], up_weight[0], scale),
        hidden_of(shared_gate, shared_up, shared_scale),
        down_weight[0],
        shared_down,
    )


def per_device(
    query_rows,
    key_rows,
    value_rows,
    residual,
    out_weight,
    norm_gain,
    router_weight,
    expert_ids,
    gate_weight,
    up_weight,
    down_weight,
    shared_gate_weight,
    shared_up_weight,
    shared_down_weight,
    shared_gate_vector,
    segment_ids,
    pad_mask,
    page_table,
):
    tokens_here = query_rows.shape[0]
    feat_width = query_rows.shape[1]
    heads_here = feat_width // HD
    seq_count = lax.axis_size("seq")
    me = lax.axis_index("seq")
    expert_count = seq_count * gate_weight.shape[0]
    per_token = expert_ids.shape[1]
    pages_here = page_table.shape[0]
    page_rows = tokens_here // pages_here
    capacity = 2 * tokens_here * per_token // expert_count
    query_heads = query_rows.reshape(tokens_here, heads_here, HD)
    kv_local = jnp.concatenate([key_rows, value_rows], 1)
    notes = jnp.concatenate([segment_ids, pad_mask, expert_ids.T.reshape(-1), page_table])
    dense = (
        capacity >= tokens_here
        and gate_weight.shape[0] == 1
        and seq_count % 2 == 0
        and lax.axis_size("tp") == 4
    )
    if dense:
        padded = -(-notes.shape[0] // 1024) * 8
        flat = jnp.pad(notes, (0, padded * 128 - notes.shape[0])).reshape(padded, 128)
        gathered_kv, all_notes, gate_split, up_split, shared_down = gather_over_seq(
            kv_local, flat, shared_gate_weight, shared_up_weight, shared_down_weight
        )
        all_notes = all_notes.reshape(seq_count, -1)[:, : notes.shape[0]]
    else:
        all_notes = lax.all_gather(notes, "seq", axis=0, tiled=False)
        gathered_kv = lax.all_gather(kv_local, "seq", axis=0, tiled=True)
    window = min(seq_count, REACH + 1)
    first = jnp.clip(me - REACH, 0, seq_count - window)
    if window == seq_count:
        all_kv, window_notes = gathered_kv, all_notes
    else:
        all_kv = lax.dynamic_slice_in_dim(gathered_kv, first * tokens_here, window * tokens_here, 0)
        window_notes = lax.dynamic_slice_in_dim(all_notes, first, window, 0)
    key_segment = window_notes[:, :tokens_here].reshape(-1)
    key_mask = window_notes[:, tokens_here : 2 * tokens_here].reshape(-1)
    query_place = (me - first) * tokens_here + jnp.arange(tokens_here, dtype=jnp.int32)
    key_place = jnp.arange(window * tokens_here, dtype=jnp.int32)
    all_visible = (
        (segment_ids[:, None] == key_segment[None, :])
        & (key_place[None, :] <= query_place[:, None])
        & ((key_mask[None, :] == 1) | (key_place[None, :] == query_place[:, None]))
    )
    key_heads = all_kv[:, :feat_width].reshape(-1, heads_here, HD)
    scores = jnp.where(all_visible[None], head_scores(query_heads, key_heads), -jnp.inf)
    row_top = jnp.max(scores, -1)
    weights_raw = jnp.exp(scores - row_top[..., None])
    row_total = jnp.sum(weights_raw, -1)
    all_values = all_kv[:, feat_width:].reshape(-1, heads_here, HD)
    mixed_heads = jnp.einsum(
        "hqk,khd->qhd",
        weights_raw.astype(jnp.bfloat16),
        all_values,
        preferred_element_type=jnp.float32,
    )
    all_slots = all_notes[:, -pages_here:].reshape(-1)
    my_slots = me * pages_here + jnp.arange(pages_here, dtype=jnp.int32)
    my_pages = jnp.argmax(all_slots[None, :] == my_slots[:, None], 1)
    kv_cache = jnp.stack(
        [
            lax.dynamic_slice_in_dim(gathered_kv, my_pages[page] * page_rows, page_rows, 0)
            for page in range(pages_here)
        ]
    )
    attended = (
        (mixed_heads / row_total.T[:, :, None])
        .astype(jnp.bfloat16)
        .reshape(tokens_here, feat_width)
    )
    if dense:
        stream, rows, shared_gate, shared_up = project_and_norm(
            attended, out_weight, residual, norm_gain, gate_split, up_split
        )
        mixed = everywhere(
            rows,
            all_notes,
            router_weight,
            shared_gate_vector,
            gate_weight,
            up_weight,
            down_weight,
            shared_gate,
            shared_up,
            shared_down,
            per_token,
        )
        return (stream + mixed, kv_cache)
    projected = jnp.dot(attended, out_weight, preferred_element_type=jnp.float32)
    projected = lax.psum_scatter(
        projected.astype(jnp.bfloat16), "tp", scatter_dimension=1, tiled=True
    ).astype(jnp.float32)
    stream = residual.astype(jnp.float32) + projected
    square_sum = lax.psum(jnp.sum(stream * stream, 1), "tp")
    normed = (
        stream * lax.rsqrt(square_sum / D + norm_eps)[:, None] * norm_gain.astype(jnp.float32)
    ).astype(jnp.bfloat16)
    full_normed = lax.all_gather(normed, "tp", axis=1, tiled=True)
    logits = jnp.dot(full_normed, router_weight, preferred_element_type=jnp.float32)
    shared_gate_act = jnp.dot(
        full_normed,
        lax.all_gather(shared_gate_weight, "seq", axis=0, tiled=True),
        preferred_element_type=jnp.float32,
    )
    shared_up_act = jnp.dot(
        full_normed,
        lax.all_gather(shared_up_weight, "seq", axis=0, tiled=True),
        preferred_element_type=jnp.float32,
    )
    shared_hidden = (jax.nn.silu(shared_gate_act) * shared_up_act).astype(jnp.bfloat16)
    shared_part = jnp.dot(
        shared_hidden,
        lax.all_gather(shared_down_weight, "seq", axis=1, tiled=True),
        preferred_element_type=jnp.float32,
    )
    shared_out = lax.psum_scatter(
        shared_part.astype(jnp.bfloat16), "tp", scatter_dimension=1, tiled=True
    ).astype(jnp.float32)
    shared_scale = jax.nn.sigmoid(
        jnp.dot(full_normed, shared_gate_vector, preferred_element_type=jnp.float32)
    )
    flat_expert = expert_ids.reshape(-1)
    expert_range = jnp.arange(expert_count, dtype=jnp.int32)
    onehot = (flat_expert[:, None] == expert_range[None, :]).astype(BF16)
    place_range = jnp.arange(flat_expert.shape[0], dtype=jnp.int32)
    earlier = (place_range[:, None] >= place_range[None, :]).astype(BF16)
    running = jnp.dot(earlier, onehot, preferred_element_type=F32)
    slot_rank = jnp.sum(running * onehot.astype(F32), 1).astype(jnp.int32) - 1
    slot_index = flat_expert * capacity + slot_rank
    token_of = jnp.arange(tokens_here * per_token, dtype=jnp.int32) // per_token
    source_row = (
        jnp.full((expert_count * capacity,), tokens_here, jnp.int32).at[slot_index].set(token_of)
    )
    slice_width = normed.shape[1]
    padded_rows = jnp.concatenate([normed, jnp.zeros((1, slice_width), jnp.bfloat16)], 0)
    outgoing = padded_rows[source_row].reshape(expert_count, capacity, slice_width)
    whole_rows = lax.all_gather(
        lax.all_to_all(outgoing, "seq", split_axis=0, concat_axis=0, tiled=True),
        "tp",
        axis=2,
        tiled=True,
    )
    returned = run_experts(whole_rows, gate_weight, up_weight, down_weight)
    chosen = expert_ids[:, :, None] == expert_range[None, None, :]
    chosen_logits = jnp.sum(jnp.where(chosen, logits[:, None, :], 0.0), 2)
    choice_top = jnp.max(chosen_logits, 1, keepdims=True)
    choice_exp = jnp.exp(chosen_logits - choice_top)
    route_weight = choice_exp / jnp.sum(choice_exp, 1, keepdims=True)
    back_rows = returned.reshape(expert_count * capacity, returned.shape[2])[slot_index]
    weighted = (
        back_rows.astype(jnp.float32).reshape(tokens_here, per_token, returned.shape[2])
        * route_weight[:, :, None]
    )
    layer_out = stream + jnp.sum(weighted, 1) + shared_scale[:, None] * shared_out
    return (layer_out, kv_cache)


def solution(mesh):
    placed = (
        P("seq", "tp"),
        P("seq", "tp"),
        P("seq", "tp"),
        P("seq", "tp"),
        P("tp", None),
        P("tp"),
        P(),
        P("seq", None),
        P("seq", None, "tp"),
        P("seq", None, "tp"),
        P("seq", "tp", None),
        P("seq", "tp"),
        P("seq", "tp"),
        P("tp", "seq"),
        P(),
        P("seq"),
        P("seq"),
        P("seq"),
    )
    return jax.shard_map(
        per_device,
        mesh=mesh,
        in_specs=placed,
        out_specs=(P("seq", "tp"), P("seq", None, "tp")),
        check_vma=False,
    )
```

```python
import functools

import jax
import jax.numpy as jnp
from jax import lax
from jax.experimental import pallas as pl
from jax.experimental.pallas import tpu as pltpu
from jax.sharding import PartitionSpec as P

D = 2048
HD = 128
REACH = 7


norm_eps = 1e-06


MESH = pl.DeviceIdType.MESH
BF16, F32 = jnp.bfloat16, jnp.float32


def place(seq_count):
    me, tp = lax.axis_index("seq"), lax.axis_index("tp")
    return me, tp, me // 2, lax.rem(me, 2), seq_count // 2


def greet(peers):
    barrier = pltpu.get_barrier_semaphore()
    for peer in peers:
        pl.semaphore_signal(barrier, inc=1, device_id=peer, device_id_type=MESH)
    pl.semaphore_wait(barrier, len(peers))


def remote(src, dst, sems, index, peer):
    copy = pltpu.make_async_remote_copy(
        src_ref=src,
        dst_ref=dst,
        send_sem=sems[0].at[index],
        recv_sem=sems[1].at[index],
        device_id=peer,
        device_id_type=MESH,
    )
    copy.start()
    return copy


def nt(left, right):
    return lax.dot_general(left, right, (((1,), (1,)), ((), ())), preferred_element_type=F32)


def maybe(condition, action):
    if condition is None:
        action()
    else:
        pl.when(condition)(action)


class Send:
    def __init__(self, src, dst, sems, index, peer, go=None, come=None):
        self.go, self.come = go, come
        self.make = lambda: pltpu.make_async_remote_copy(
            src_ref=src,
            dst_ref=dst,
            send_sem=sems[0].at[index],
            recv_sem=sems[1].at[index],
            device_id=peer,
            device_id_type=MESH,
        )

    def start(self):
        maybe(self.go, lambda: self.make().start())
        return self

    def wait_recv(self):
        maybe(self.come, lambda: self.make().wait_recv())

    def wait_send(self):
        maybe(self.go, lambda: self.make().wait_send())


def both(first, second):
    if first is None:
        return second
    if second is None:
        return first
    return jnp.logical_and(first, second)


def layer_kernel(
    seq_count,
    per_token,
    query,
    key,
    value,
    notes,
    shared_gate,
    shared_up,
    shared_down,
    out_weight,
    residual,
    gain,
    router,
    gate,
    up,
    down,
    out,
    all_kv,
    all_notes,
    query_v,
    kv,
    raw_gate,
    raw_up,
    turned_gate,
    turned_up,
    gate_full,
    up_full,
    down_full,
    out_weight_v,
    residual_v,
    gain_v,
    router_v,
    gate_v,
    up_v,
    down_v,
    bias,
    attended,
    part_out,
    part_in,
    stream,
    square_out,
    square_in,
    square_all,
    mine,
    rows,
    hidden,
    shared_hidden,
    core_out,
    core_in,
    far_out,
    far_in,
    pair_out,
    pair_in,
    down_out,
    down_in,
    kept,
    half,
    local,
    kv_send,
    kv_recv,
    note_send,
    note_recv,
    swap_send,
    swap_recv,
    tp_send,
    tp_recv,
    row_send,
    row_recv,
    red_send,
    red_recv,
):
    me, tp, z, x, groups = place(seq_count)
    tokens, width = query.shape
    depth = shared_gate.shape[0]
    units = shared_gate.shape[1] // seq_count
    heads = width // HD
    y, c = tp // 2, lax.rem(tp, 2)
    others = [lax.rem(me + k, seq_count) for k in range(1, seq_count)]
    row_peers = [(me, lax.rem(tp + k, 4)) for k in range(1, 4)]
    pair = (z * 2 + 1 - x, tp)
    core = (me, y * 2 + 1 - c)
    far = (me, lax.rem(tp + 2, 4))
    column = [(lax.rem(z + k, groups) * 2 + x, tp) for k in range(1, groups)]
    nexts = [(lax.rem(z + 1, groups) * 2 + x, tp), (lax.rem(z + groups - 1, groups) * 2 + x, tp)]
    beyond = [z + 1 < groups, z >= 1]
    slots = [(0, 0)] + [(way, j) for j in range(1, groups) for way in range(2)]
    count = len(slots)
    sent = []

    def exists(way, j):
        if j == 0:
            return None
        return z >= j if way == 0 else z + j < groups

    def origin(way, j):
        return lax.rem(z + groups - j, groups) if way == 0 else lax.rem(z + j, groups)

    def rows_of(owner):
        return pl.ds(pl.multiple_of(owner * tokens, tokens), tokens)

    def cols_of(tp_owner):
        return pl.ds(pl.multiple_of(tp_owner * width, width), width)

    own_depth = pl.ds(pl.multiple_of(me * depth, depth), depth)

    def unit_rows(owner):
        return pl.ds(pl.multiple_of(owner * units, units), units)

    def kv_view(piece, owner):
        return kv.at[rows_of(owner), pl.ds(piece * width, width)]

    loads = [
        (query, query_v),
        (key, kv_view(0, me)),
        (value, kv_view(1, me)),
        (notes, all_notes.at[me]),
        (shared_gate, raw_gate),
        (shared_up, raw_up),
        (shared_down.at[unit_rows(me), :], down_full.at[:, own_depth]),
        (out_weight, out_weight_v),
        (residual, residual_v),
        (gain, gain_v),
        (router, router_v),
        (gate, gate_v),
        (up, up_v),
        (down, down_v),
    ]
    loads = [pltpu.make_async_copy(a, b, local.at[i]) for i, (a, b) in enumerate(loads)]
    for copy in loads:
        copy.start()
    greet([(other, tp) for other in others] + row_peers)

    kv_sems = (kv_send, kv_recv)

    def kv_hop(way, j, piece, source=None):
        block = kv_view(piece, origin(way, j) * 2 + x)
        index = (piece * 2 + way) * (groups - 1) + j
        return Send(
            block if source is None else source,
            block,
            kv_sems,
            index,
            nexts[way],
            both(exists(way, j), beyond[way]),
            exists(way, j + 1),
        )

    def kv_across(way, j, piece, source=None):
        block = kv_view(piece, origin(way, j) * 2 + x)
        index = 4 * (groups - 1) + piece * count + slots.index((way, j))
        return Send(
            block if source is None else source,
            block,
            kv_sems,
            index,
            pair,
            exists(way, j),
            exists(way, j),
        )

    def go(copy):
        sent.append(copy.start())
        return copy

    hop, across = {}, {}
    for piece, source in enumerate((key, value)):
        for way in range(2):
            hop[way, 0, piece] = go(kv_hop(way, 0, piece, source))
        across[0, 0, piece] = go(kv_across(0, 0, piece, source))
    note_sems = (note_send, note_recv)
    note_copies = [
        go(Send(notes, all_notes.at[me], note_sems, i, (other, tp)))
        for i, other in enumerate(others)
    ]
    swap_sems = (swap_send, swap_recv)
    swaps = []

    def swap(which, source, target):
        for i, other in enumerate(others):
            swaps.append(
                go(
                    Send(
                        source.at[unit_rows(other), :],
                        target.at[:, own_depth],
                        swap_sems,
                        which * (seq_count - 1) + i,
                        (other, tp),
                    )
                )
            )

    def turn(raw, turned, full):
        for start in range(0, raw.shape[1], 128):
            turned[start : start + 128, :] = raw[:, start : start + 128].T
        full[:, own_depth] = turned[unit_rows(me), :]

    def relay(j):
        for way in range(2):
            for piece in range(2):
                hop[way, j - 1, piece].wait_recv()
                if j < groups - 1:
                    hop[way, j, piece] = go(kv_hop(way, j, piece))
                across[way, j, piece] = go(kv_across(way, j, piece))

    loads[4].wait()
    turn(raw_gate, turned_gate, gate_full)
    relay(1)
    loads[5].wait()
    turn(raw_up, turned_up, up_full)
    swap(0, shared_down, down_full)
    for j in range(2, groups):
        relay(j)
    swap(1, turned_gate, gate_full)

    for i in (0, 1, 2, 3):
        loads[i].wait()
    for copy in note_copies:
        copy.wait_recv()
    own_segment = all_notes[me].T[:, 0:1]
    query_place = me * tokens + lax.broadcasted_iota(jnp.int32, (tokens, tokens), 0)
    for owner in range(seq_count):
        key_place = owner * tokens + lax.broadcasted_iota(jnp.int32, (tokens, tokens), 1)
        seen = (
            (own_segment == all_notes[owner, 0:1, :])
            & (key_place <= query_place)
            & ((all_notes[owner, 1:2, :] == 1) | (key_place == query_place))
        )
        bias[:, owner * tokens : (owner + 1) * tokens] = jnp.where(seen, 0.0, -jnp.inf)

    for copy in across.values():
        copy.wait_recv()
    keep = pltpu.make_async_copy(kv, all_kv, local.at[len(loads)])
    keep.start()
    swap(2, turned_up, up_full)
    for head in range(heads):
        cols = slice(head * HD, (head + 1) * HD)
        scores = nt(query_v[:, cols], kv[:, cols]) * HD**-0.5 + bias[...]
        raw = jnp.exp(scores - jnp.max(scores, 1, keepdims=True))
        total = jnp.sum(raw, 1, keepdims=True)
        values = kv[:, width + head * HD : width + (head + 1) * HD]
        mixed = jnp.dot(raw.astype(BF16), values, preferred_element_type=F32)
        attended[:, cols] = (mixed / total).astype(BF16)

    tp_sems = (tp_send, tp_recv)
    for i in (7, 8, 9):
        loads[i].wait()

    def part(owner):
        return jnp.dot(attended[...], out_weight_v[:, cols_of(owner)], preferred_element_type=F32)

    copies = []
    for k in (2, 1, 3):
        part_out[k - 1] = part(lax.rem(tp + k, 4)).astype(BF16)
        copies.append(
            go(Send(part_out.at[k - 1], part_in.at[k - 1], tp_sems, k - 1, row_peers[k - 1]))
        )
    total = residual_v[...].astype(F32) + part(tp)
    for copy in copies:
        copy.wait_recv()
    for k in range(3):
        total += part_in[k].astype(F32)
    stream[...] = total
    mine[...] = (total * gain_v[...].astype(F32)).astype(BF16)

    row_sems = (row_send, row_recv)

    def row_view(owner, tp_owner):
        return rows.at[rows_of(owner), cols_of(tp_owner)]

    def row_hop(way, j, source=None):
        block = row_view(origin(way, j) * 2 + x, tp)
        return Send(
            block if source is None else source,
            block,
            row_sems,
            way * (groups - 1) + j,
            nexts[way],
            both(exists(way, j), beyond[way]),
            exists(way, j + 1),
        )

    def row_copy(kind, way, j, peer, other_x, other_y, source=None):
        owner = origin(way, j) * 2 + (1 - x if other_x else x)
        block = row_view(owner, lax.rem(tp + 2, 4) if other_y else tp)
        index = 2 * (groups - 1) + kind * count + slots.index((way, j))
        ok = exists(way, j)
        return go(Send(block if source is None else source, block, row_sems, index, peer, ok, ok))

    hop, across, over, diag, near = {}, {}, {}, {}, []

    def spread(way, j, source=None):
        across[way, j] = row_copy(0, way, j, pair, False, False, source)
        over[way, j] = row_copy(1, way, j, far, False, False, source)
        near.append(row_copy(3, way, j, core, False, False, source))

    for way in range(2):
        hop[way, 0] = go(row_hop(way, 0, mine))
    spread(0, 0, mine)
    place_mine = pltpu.make_async_copy(mine, row_view(me, tp), local.at[len(loads) + 1])
    place_mine.start()

    squares = jnp.sum(total * total, 1, keepdims=True)
    own_squares = jnp.broadcast_to(squares, (tokens, tokens)).T[0:8, :]
    square_out[0] = own_squares
    square_copies = [
        go(Send(square_out.at[0], square_in.at[k], tp_sems, 3 + k, row_peers[k])) for k in range(3)
    ]
    for copy in square_copies:
        copy.wait_recv()
    own_squares = own_squares + square_in[0] + square_in[1] + square_in[2]
    square_out[1] = own_squares
    square_all[me] = own_squares
    square_copies = [
        go(Send(square_out.at[1], square_all.at[me], tp_sems, 6 + i, (other, tp)))
        for i, other in enumerate(others)
    ]

    for j in range(1, groups):
        for way in range(2):
            hop[way, j - 1].wait_recv()
            if j < groups - 1:
                hop[way, j] = go(row_hop(way, j))
            spread(way, j)
    for way, j in slots:
        across[way, j].wait_recv()
        near.append(row_copy(4, way, j, core, True, False))
        if j % 2 == 1:
            diag[way, j] = row_copy(2, way, j, far, True, False)
        over[way, j].wait_recv()
        near.append(row_copy(5, way, j, core, False, True))
        if j % 2 == 0:
            diag[way, j] = row_copy(2, way, j, pair, False, True)
    for way, j in slots:
        diag[way, j].wait_recv()
        near.append(row_copy(6, way, j, core, True, True))
    place_mine.wait()
    for copy in square_copies + near:
        copy.wait_recv()
    for i in (10, 11, 12, 13):
        loads[i].wait()
    loads[6].wait()
    for copy in swaps:
        copy.wait_recv()

    red_sems = (red_send, red_recv)
    first_far, first_pair, first_down = 2 * groups, 3 * groups, 4 * groups
    lanes = lax.broadcasted_iota(jnp.int32, (tokens, router.shape[0]), 1)

    def chunk(k):
        return pl.ds(pl.multiple_of(lax.rem(z + k, groups) * 2 * tokens, 2 * tokens), 2 * tokens)

    def scales(owner, logits, inverse):
        ids = all_notes[owner].T
        chosen = lanes == ids[:, 2:3]
        for k in range(1, per_token):
            chosen = chosen | (lanes == ids[:, 2 + k : 3 + k])
        logits = logits * inverse
        top = jnp.max(jnp.where(chosen, logits, -jnp.inf), 1, keepdims=True)
        raw = jnp.where(chosen, jnp.exp(logits - top), 0.0)
        route = jnp.sum(jnp.where(lanes == me, raw, 0.0), 1, keepdims=True) / jnp.sum(
            raw, 1, keepdims=True
        )
        share = jax.nn.sigmoid(logits[:, seq_count : seq_count + 1])
        return route, share

    def fill(k):
        block = rows[chunk(k), :]
        logits = nt(block, router_v[...])
        first = lax.rem(z + k, groups) * 2
        inverses, routes, shares = [], [], []
        for i in range(2):
            squares = square_all[first + i].T[:, 0:1]
            inverse = lax.rsqrt(squares / D + norm_eps)
            route, share = scales(first + i, logits[i * tokens : (i + 1) * tokens], inverse)
            inverses.append(inverse)
            routes.append(route)
            shares.append(share)
        inverse = jnp.concatenate(inverses, 0)

        def hide(gates, ups, factor):
            return (
                jax.nn.silu(nt(block, gates) * inverse) * (nt(block, ups) * inverse) * factor
            ).astype(BF16)

        hidden[chunk(k), :] = hide(gate_v[...], up_v[...], jnp.concatenate(routes, 0))
        shared_hidden[chunk(k), :] = hide(gate_full[...], up_full[...], jnp.concatenate(shares, 0))

    def product(k, tp_owner):
        return jnp.dot(
            hidden[chunk(k), :], down_v[:, cols_of(tp_owner)], preferred_element_type=F32
        ) + jnp.dot(
            shared_hidden[chunk(k), :],
            down_full[:, cols_of(tp_owner)],
            preferred_element_type=F32,
        )

    order = list(range(1, groups)) + [0]
    to_core, to_far, to_pair, to_down = {}, {}, {}, []

    def start_core(k):
        fill(k)
        to_core[k] = []
        for side in range(2):
            core_out[k, side] = product(k, side * 2 + 1 - c).astype(BF16)
            to_core[k].append(
                go(
                    Send(
                        core_out.at[k, side], core_in.at[k, side], red_sems, 2 * k + side, core
                    )
                )
            )

    start_core(order[0])
    for step in range(groups + 2):
        if step + 1 < groups:
            start_core(order[step + 1])
        if step < groups:
            k = order[step]
            away_y = product(k, (1 - y) * 2 + c)
            kept[k] = product(k, tp)
            for copy in to_core[k]:
                copy.wait_recv()
            far_out[k] = (away_y + core_in[k, 1 - y].astype(F32)).astype(BF16)
            to_far[k] = go(Send(far_out.at[k], far_in.at[k], red_sems, first_far + k, far))
            kept[k] = kept[k] + core_in[k, y].astype(F32)
        if 0 <= step - 1 < groups:
            k = order[step - 1]
            to_far[k].wait_recv()
            kept[k] = kept[k] + far_in[k].astype(F32)
            pair_out[k] = kept[k, rows_of(1 - x), :].astype(BF16)
            to_pair[k] = go(Send(pair_out.at[k], pair_in.at[k], red_sems, first_pair + k, pair))
        if 0 <= step - 2 < groups:
            k = order[step - 2]
            to_pair[k].wait_recv()
            amount = kept[k, rows_of(x), :] + pair_in[k].astype(F32)
            if k == 0:
                half[...] = amount
            else:
                down_out[k - 1] = amount.astype(BF16)
                to_down.append(
                    go(
                        Send(
                            down_out.at[k - 1],
                            down_in.at[k - 1],
                            red_sems,
                            first_down + k - 1,
                            column[k - 1],
                        )
                    )
                )
    for copy in to_down:
        copy.wait_recv()
    amount = stream[...] + half[...]
    for k in range(groups - 1):
        amount += down_in[k].astype(F32)
    out[...] = amount
    for copy in sent:
        copy.wait_send()
    keep.wait()


def whole_layer(
    query,
    key,
    value,
    notes,
    shared_gate,
    shared_up,
    shared_down,
    out_weight,
    residual,
    gain,
    router,
    gate,
    up,
    down,
    per_token,
):
    seq_count = lax.axis_size("seq")
    groups = seq_count // 2
    tokens, width = query.shape
    depth, all_units = shared_gate.shape
    units = all_units // seq_count
    total, features = seq_count * tokens, 4 * width
    count = 2 * groups - 1
    hops = 2 * (groups - 1)

    def vmem(*shape, dtype=BF16):
        return pltpu.VMEM(shape, dtype)

    def sems(number):
        return [pltpu.SemaphoreType.DMA((number,))] * 2

    return pl.pallas_call(
        functools.partial(layer_kernel, seq_count, per_token),
        out_shape=(
            jax.ShapeDtypeStruct((tokens, width), F32),
            jax.ShapeDtypeStruct((total, 2 * width), BF16),
            jax.ShapeDtypeStruct((seq_count, 8, tokens), jnp.int32),
        ),
        in_specs=[pl.BlockSpec(memory_space=pl.ANY)] * 14,
        out_specs=(
            pl.BlockSpec(memory_space=pltpu.VMEM),
            pl.BlockSpec(memory_space=pl.ANY),
            pl.BlockSpec(memory_space=pltpu.VMEM),
        ),
        scratch_shapes=[
            vmem(tokens, width),
            vmem(total, 2 * width),
            vmem(depth, all_units),
            vmem(depth, all_units),
            vmem(all_units, depth),
            vmem(all_units, depth),
            vmem(units, features),
            vmem(units, features),
            vmem(units, features),
            vmem(*out_weight.shape),
            vmem(tokens, width),
            vmem(1, width),
            vmem(*router.shape),
            vmem(*gate.shape),
            vmem(*up.shape),
            vmem(*down.shape),
            vmem(tokens, total, dtype=F32),
            vmem(tokens, width),
            vmem(3, tokens, width),
            vmem(3, tokens, width),
            vmem(tokens, width, dtype=F32),
            vmem(2, 8, tokens, dtype=F32),
            vmem(3, 8, tokens, dtype=F32),
            vmem(seq_count, 8, tokens, dtype=F32),
            vmem(tokens, width),
            vmem(total, features),
            vmem(total, gate.shape[0]),
            vmem(total, units),
            vmem(groups, 2, 2 * tokens, width),
            vmem(groups, 2, 2 * tokens, width),
            vmem(groups, 2 * tokens, width),
            vmem(groups, 2 * tokens, width),
            vmem(groups, tokens, width),
            vmem(groups, tokens, width),
            vmem(groups - 1, tokens, width),
            vmem(groups - 1, tokens, width),
            vmem(groups, 2 * tokens, width, dtype=F32),
            vmem(tokens, width, dtype=F32),
            pltpu.SemaphoreType.DMA((16,)),
        ]
        + sems(2 * (hops + count))
        + sems(seq_count - 1)
        + sems(3 * (seq_count - 1))
        + sems(6 + seq_count - 1)
        + sems(hops + 7 * count)
        + sems(5 * groups - 1),
        compiler_params=pltpu.CompilerParams(
            collective_id=0, has_side_effects=True, vmem_limit_bytes=56 * 2**20
        ),
        cost_estimate=pl.CostEstimate(
            flops=8_000_000_000, transcendentals=1_000_000, bytes_accessed=30_000_000
        ),
    )(
        query,
        key,
        value,
        notes,
        shared_gate,
        shared_up,
        shared_down,
        out_weight,
        residual,
        gain,
        router,
        gate,
        up,
        down,
    )


def head_scores(query_heads, key_heads):
    score_scale = query_heads.shape[-1] ** (-0.5)
    return (
        jnp.einsum("qhd,khd->hqk", query_heads, key_heads, preferred_element_type=jnp.float32)
        * score_scale
    )


def run_experts(rows_in, gate_weight, up_weight, down_weight):
    local_experts = gate_weight.shape[0]
    sources = rows_in.shape[0] // local_experts
    grouped = rows_in.reshape(sources, local_experts, rows_in.shape[1], rows_in.shape[2])
    gate_act = jnp.einsum(
        "nesd,edf->nesf", grouped, gate_weight, preferred_element_type=jnp.float32
    )
    up_act = jnp.einsum("nesd,edf->nesf", grouped, up_weight, preferred_element_type=jnp.float32)
    hidden = (jax.nn.silu(gate_act) * up_act).astype(jnp.bfloat16)
    partial_out = jnp.einsum(
        "nesf,efd->nesd", hidden, down_weight, preferred_element_type=jnp.float32
    )
    partial_out = partial_out.reshape(rows_in.shape[0], rows_in.shape[1], down_weight.shape[2])
    summed = lax.psum_scatter(
        partial_out.astype(jnp.bfloat16), "tp", scatter_dimension=2, tiled=True
    )
    return lax.all_to_all(summed, "seq", split_axis=0, concat_axis=0, tiled=True)


def per_device(
    query_rows,
    key_rows,
    value_rows,
    residual,
    out_weight,
    norm_gain,
    router_weight,
    expert_ids,
    gate_weight,
    up_weight,
    down_weight,
    shared_gate_weight,
    shared_up_weight,
    shared_down_weight,
    shared_gate_vector,
    segment_ids,
    pad_mask,
    page_table,
):
    tokens_here = query_rows.shape[0]
    feat_width = query_rows.shape[1]
    heads_here = feat_width // HD
    seq_count = lax.axis_size("seq")
    me = lax.axis_index("seq")
    expert_count = seq_count * gate_weight.shape[0]
    per_token = expert_ids.shape[1]
    pages_here = page_table.shape[0]
    page_rows = tokens_here // pages_here
    capacity = 2 * tokens_here * per_token // expert_count
    query_heads = query_rows.reshape(tokens_here, heads_here, HD)
    dense = (
        capacity >= tokens_here
        and gate_weight.shape[0] == 1
        and seq_count % 2 == 0
        and lax.axis_size("tp") == 4
        and per_token <= 5
        and seq_count <= 15
    )
    if dense:
        rows = [segment_ids[None], pad_mask[None], expert_ids.T]
        rows.append(jnp.pad(page_table, (0, tokens_here - pages_here))[None])
        rows.append(jnp.zeros((5 - per_token, tokens_here), jnp.int32))
        router = jnp.concatenate(
            [
                router_weight.T,
                shared_gate_vector[None],
                jnp.zeros((15 - seq_count, D), BF16),
            ]
        )
        layer_out, all_kv, all_notes = whole_layer(
            query_rows,
            key_rows,
            value_rows,
            jnp.concatenate(rows),
            shared_gate_weight,
            shared_up_weight,
            shared_down_weight,
            out_weight,
            residual,
            norm_gain.reshape(1, feat_width),
            router,
            gate_weight[0].T,
            up_weight[0].T,
            down_weight[0],
            per_token,
        )
        all_slots = all_notes[:, 2 + per_token, :pages_here].reshape(-1)
        my_slots = me * pages_here + jnp.arange(pages_here, dtype=jnp.int32)
        my_pages = jnp.argmax(all_slots[None, :] == my_slots[:, None], 1)
        kv_cache = jnp.stack(
            [
                lax.dynamic_slice_in_dim(all_kv, my_pages[page] * page_rows, page_rows, 0)
                for page in range(pages_here)
            ]
        )
        return layer_out, kv_cache
    kv_local = jnp.concatenate([key_rows, value_rows], 1)
    notes = jnp.concatenate([segment_ids, pad_mask, expert_ids.T.reshape(-1), page_table])
    all_notes = lax.all_gather(notes, "seq", axis=0, tiled=False)
    gathered_kv = lax.all_gather(kv_local, "seq", axis=0, tiled=True)
    window = min(seq_count, REACH + 1)
    first = jnp.clip(me - REACH, 0, seq_count - window)
    if window == seq_count:
        all_kv, window_notes = gathered_kv, all_notes
    else:
        all_kv = lax.dynamic_slice_in_dim(gathered_kv, first * tokens_here, window * tokens_here, 0)
        window_notes = lax.dynamic_slice_in_dim(all_notes, first, window, 0)
    key_segment = window_notes[:, :tokens_here].reshape(-1)
    key_mask = window_notes[:, tokens_here : 2 * tokens_here].reshape(-1)
    query_place = (me - first) * tokens_here + jnp.arange(tokens_here, dtype=jnp.int32)
    key_place = jnp.arange(window * tokens_here, dtype=jnp.int32)
    all_visible = (
        (segment_ids[:, None] == key_segment[None, :])
        & (key_place[None, :] <= query_place[:, None])
        & ((key_mask[None, :] == 1) | (key_place[None, :] == query_place[:, None]))
    )
    key_heads = all_kv[:, :feat_width].reshape(-1, heads_here, HD)
    scores = jnp.where(all_visible[None], head_scores(query_heads, key_heads), -jnp.inf)
    row_top = jnp.max(scores, -1)
    weights_raw = jnp.exp(scores - row_top[..., None])
    row_total = jnp.sum(weights_raw, -1)
    all_values = all_kv[:, feat_width:].reshape(-1, heads_here, HD)
    mixed_heads = jnp.einsum(
        "hqk,khd->qhd",
        weights_raw.astype(jnp.bfloat16),
        all_values,
        preferred_element_type=jnp.float32,
    )
    all_slots = all_notes[:, -pages_here:].reshape(-1)
    my_slots = me * pages_here + jnp.arange(pages_here, dtype=jnp.int32)
    my_pages = jnp.argmax(all_slots[None, :] == my_slots[:, None], 1)
    kv_cache = jnp.stack(
        [
            lax.dynamic_slice_in_dim(gathered_kv, my_pages[page] * page_rows, page_rows, 0)
            for page in range(pages_here)
        ]
    )
    attended = (
        (mixed_heads / row_total.T[:, :, None])
        .astype(jnp.bfloat16)
        .reshape(tokens_here, feat_width)
    )
    projected = jnp.dot(attended, out_weight, preferred_element_type=jnp.float32)
    projected = lax.psum_scatter(
        projected.astype(jnp.bfloat16), "tp", scatter_dimension=1, tiled=True
    ).astype(jnp.float32)
    stream = residual.astype(jnp.float32) + projected
    square_sum = lax.psum(jnp.sum(stream * stream, 1), "tp")
    normed = (
        stream * lax.rsqrt(square_sum / D + norm_eps)[:, None] * norm_gain.astype(jnp.float32)
    ).astype(jnp.bfloat16)
    full_normed = lax.all_gather(normed, "tp", axis=1, tiled=True)
    logits = jnp.dot(full_normed, router_weight, preferred_element_type=jnp.float32)
    shared_gate_act = jnp.dot(
        full_normed,
        lax.all_gather(shared_gate_weight, "seq", axis=0, tiled=True),
        preferred_element_type=jnp.float32,
    )
    shared_up_act = jnp.dot(
        full_normed,
        lax.all_gather(shared_up_weight, "seq", axis=0, tiled=True),
        preferred_element_type=jnp.float32,
    )
    shared_hidden = (jax.nn.silu(shared_gate_act) * shared_up_act).astype(jnp.bfloat16)
    shared_part = jnp.dot(
        shared_hidden,
        lax.all_gather(shared_down_weight, "seq", axis=1, tiled=True),
        preferred_element_type=jnp.float32,
    )
    shared_out = lax.psum_scatter(
        shared_part.astype(jnp.bfloat16), "tp", scatter_dimension=1, tiled=True
    ).astype(jnp.float32)
    shared_scale = jax.nn.sigmoid(
        jnp.dot(full_normed, shared_gate_vector, preferred_element_type=jnp.float32)
    )
    flat_expert = expert_ids.reshape(-1)
    expert_range = jnp.arange(expert_count, dtype=jnp.int32)
    onehot = (flat_expert[:, None] == expert_range[None, :]).astype(BF16)
    place_range = jnp.arange(flat_expert.shape[0], dtype=jnp.int32)
    earlier = (place_range[:, None] >= place_range[None, :]).astype(BF16)
    running = jnp.dot(earlier, onehot, preferred_element_type=F32)
    slot_rank = jnp.sum(running * onehot.astype(F32), 1).astype(jnp.int32) - 1
    slot_index = flat_expert * capacity + slot_rank
    token_of = jnp.arange(tokens_here * per_token, dtype=jnp.int32) // per_token
    source_row = (
        jnp.full((expert_count * capacity,), tokens_here, jnp.int32).at[slot_index].set(token_of)
    )
    slice_width = normed.shape[1]
    padded_rows = jnp.concatenate([normed, jnp.zeros((1, slice_width), jnp.bfloat16)], 0)
    outgoing = padded_rows[source_row].reshape(expert_count, capacity, slice_width)
    whole_rows = lax.all_gather(
        lax.all_to_all(outgoing, "seq", split_axis=0, concat_axis=0, tiled=True),
        "tp",
        axis=2,
        tiled=True,
    )
    returned = run_experts(whole_rows, gate_weight, up_weight, down_weight)
    chosen = expert_ids[:, :, None] == expert_range[None, None, :]
    chosen_logits = jnp.sum(jnp.where(chosen, logits[:, None, :], 0.0), 2)
    choice_top = jnp.max(chosen_logits, 1, keepdims=True)
    choice_exp = jnp.exp(chosen_logits - choice_top)
    route_weight = choice_exp / jnp.sum(choice_exp, 1, keepdims=True)
    back_rows = returned.reshape(expert_count * capacity, returned.shape[2])[slot_index]
    weighted = (
        back_rows.astype(jnp.float32).reshape(tokens_here, per_token, returned.shape[2])
        * route_weight[:, :, None]
    )
    layer_out = stream + jnp.sum(weighted, 1) + shared_scale[:, None] * shared_out
    return (layer_out, kv_cache)


def solution(mesh):
    placed = (
        P("seq", "tp"),
        P("seq", "tp"),
        P("seq", "tp"),
        P("seq", "tp"),
        P("tp", None),
        P("tp"),
        P(),
        P("seq", None),
        P("seq", None, "tp"),
        P("seq", None, "tp"),
        P("seq", "tp", None),
        P("seq", "tp"),
        P("seq", "tp"),
        P("tp", "seq"),
        P(),
        P("seq"),
        P("seq"),
        P("seq"),
    )
    return jax.shard_map(
        per_device,
        mesh=mesh,
        in_specs=placed,
        out_specs=(P("seq", "tp"), P("seq", None, "tp")),
        check_vma=False,
    )
```

```python
import functools

import jax
import jax.numpy as jnp
from jax import lax
from jax.experimental import pallas as pl
from jax.experimental.pallas import tpu as pltpu
from jax.sharding import PartitionSpec as P

D = 2048
HD = 128
REACH = 7


norm_eps = 1e-06


MESH = pl.DeviceIdType.MESH
BF16, F32 = jnp.bfloat16, jnp.float32


PLAN = {
    "sent": 0,
    "relay1": 0,
    "relay2": 0,
    "relay3": 0,
    "attend": 4,
    "project": 0,
    "rows1": 0,
    "rows2": 0,
    "rows3": 4,
    "slot": 3,
    "rest": 21,
}


def place(seq_count):
    me, tp = lax.axis_index("seq"), lax.axis_index("tp")
    return me, tp, me // 2, lax.rem(me, 2), seq_count // 2


def greet(peers):
    barrier = pltpu.get_barrier_semaphore()
    for peer in peers:
        pl.semaphore_signal(barrier, inc=1, device_id=peer, device_id_type=MESH)
    pl.semaphore_wait(barrier, len(peers))


def remote(src, dst, sems, index, peer):
    copy = pltpu.make_async_remote_copy(
        src_ref=src,
        dst_ref=dst,
        send_sem=sems[0].at[index],
        recv_sem=sems[1].at[index],
        device_id=peer,
        device_id_type=MESH,
    )
    copy.start()
    return copy


def nt(left, right):
    return lax.dot_general(left, right, (((1,), (1,)), ((), ())), preferred_element_type=F32)


def maybe(condition, action):
    if condition is None:
        action()
    else:
        pl.when(condition)(action)


class Send:
    def __init__(self, src, dst, sems, index, peer, go=None, come=None):
        self.go, self.come = go, come
        self.make = lambda: pltpu.make_async_remote_copy(
            src_ref=src,
            dst_ref=dst,
            send_sem=sems[0].at[index],
            recv_sem=sems[1].at[index],
            device_id=peer,
            device_id_type=MESH,
        )

    def start(self):
        maybe(self.go, lambda: self.make().start())
        return self

    def wait_recv(self):
        maybe(self.come, lambda: self.make().wait_recv())

    def wait_send(self):
        maybe(self.go, lambda: self.make().wait_send())


def both(first, second):
    if first is None:
        return second
    if second is None:
        return first
    return jnp.logical_and(first, second)


def layer_kernel(
    seq_count,
    per_token,
    query,
    key,
    value,
    segments,
    pads,
    choices,
    pages,
    shared_gate,
    shared_up,
    shared_down,
    out_weight,
    residual,
    gain,
    router,
    shared_vector,
    gate,
    up,
    down,
    stream,
    out,
    kv_pages,
    all_notes,
    segments_v,
    pads_v,
    choices_v,
    pages_s,
    query_v,
    kv,
    raw_gate,
    raw_up,
    turned_gate,
    turned_up,
    gate_full,
    up_full,
    down_full,
    out_weight_v,
    residual_v,
    gain_v,
    router_in,
    vector_v,
    router_v,
    gate_v,
    up_v,
    down_v,
    bias,
    attended,
    part_out,
    part_in,
    square_out,
    square_in,
    square_all,
    mine,
    rows,
    hidden,
    shared_hidden,
    core_out,
    core_in,
    far_out,
    far_in,
    pair_out,
    pair_in,
    far_more_out,
    far_more_in,
    pair_more_out,
    pair_more_in,
    down_out,
    down_in,
    kept,
    passed,
    half,
    local,
    kv_send,
    kv_recv,
    note_send,
    note_recv,
    swap_send,
    swap_recv,
    tp_send,
    tp_recv,
    row_send,
    row_recv,
    red_send,
    red_recv,
):
    me, tp, z, x, groups = place(seq_count)
    tokens, width = query.shape
    depth = shared_gate.shape[0]
    units = shared_gate.shape[1] // seq_count
    heads = width // HD
    y, c = tp // 2, lax.rem(tp, 2)
    others = [lax.rem(me + k, seq_count) for k in range(1, seq_count)]
    row_peers = [(me, lax.rem(tp + k, 4)) for k in range(1, 4)]
    pair = (z * 2 + 1 - x, tp)
    core = (me, y * 2 + 1 - c)
    far = (me, lax.rem(tp + 2, 4))
    column = [(lax.rem(z + k, groups) * 2 + x, tp) for k in range(1, groups)]
    nexts = [(lax.rem(z + 1, groups) * 2 + x, tp), (lax.rem(z + groups - 1, groups) * 2 + x, tp)]
    beyond = [z + 1 < groups, z >= 1]
    slots = [(0, 0)] + [(way, j) for j in range(1, groups) for way in range(2)]
    count = len(slots)
    sent = []

    def exists(way, j):
        if j == 0:
            return None
        return z >= j if way == 0 else z + j < groups

    def origin(way, j):
        return lax.rem(z + groups - j, groups) if way == 0 else lax.rem(z + j, groups)

    def rows_of(owner):
        return pl.ds(pl.multiple_of(owner * tokens, tokens), tokens)

    def cols_of(tp_owner):
        return pl.ds(pl.multiple_of(tp_owner * width, width), width)

    own_depth = pl.ds(pl.multiple_of(me * depth, depth), depth)

    def unit_rows(owner):
        return pl.ds(pl.multiple_of(owner * units, units), units)

    def kv_view(piece, owner):
        return kv.at[rows_of(owner), pl.ds(piece * width, width)]

    loads = [
        (query, query_v),
        (key, kv_view(0, me)),
        (value, kv_view(1, me)),
        (segments, segments_v),
        (shared_gate, raw_gate),
        (shared_up, raw_up),
        (shared_down.at[unit_rows(me), :], down_full.at[:, own_depth]),
        (out_weight, out_weight_v),
        (residual, residual_v),
        (gain, gain_v),
        (router, router_in),
        (gate, gate_v),
        (up, up_v),
        (down, down_v),
        (pads, pads_v),
        (choices, choices_v),
        (pages, pages_s),
        (shared_vector, vector_v),
    ]
    loads = [pltpu.make_async_copy(a, b, local.at[i]) for i, (a, b) in enumerate(loads)]
    for copy in loads:
        copy.start()
    greet([(other, tp) for other in others] + row_peers)

    kv_sems = (kv_send, kv_recv)

    def kv_hop(way, j, piece, source=None):
        block = kv_view(piece, origin(way, j) * 2 + x)
        index = (piece * 2 + way) * (groups - 1) + j
        return Send(
            block if source is None else source,
            block,
            kv_sems,
            index,
            nexts[way],
            both(exists(way, j), beyond[way]),
            exists(way, j + 1),
        )

    def kv_across(way, j, piece, source=None):
        block = kv_view(piece, origin(way, j) * 2 + x)
        index = 4 * (groups - 1) + piece * count + slots.index((way, j))
        return Send(
            block if source is None else source,
            block,
            kv_sems,
            index,
            pair,
            exists(way, j),
            exists(way, j),
        )

    def go(copy):
        sent.append(copy.start())
        return copy

    hop, across = {}, {}
    for piece, source in enumerate((key, value)):
        for way in range(2):
            hop[way, 0, piece] = go(kv_hop(way, 0, piece, source))
        across[0, 0, piece] = go(kv_across(0, 0, piece, source))
    note_sems = (note_send, note_recv)
    for i in (3, 14, 15, 16):
        loads[i].wait()
    page_lane = lax.broadcasted_iota(jnp.int32, (1, tokens), 1)
    page_row = jnp.zeros((1, tokens), jnp.int32)
    for i in range(pages.shape[0]):
        page_row = jnp.where(page_lane // kv_pages.shape[1] == i, pages_s[i], page_row)
    all_notes[me] = jnp.concatenate(
        [
            segments_v[...].reshape(1, tokens),
            pads_v[...].reshape(1, tokens),
            choices_v[...],
            page_row,
            jnp.zeros((5 - per_token, tokens), jnp.int32),
        ]
    )
    note_copies = [
        go(Send(all_notes.at[me], all_notes.at[me], note_sems, i, (other, tp)))
        for i, other in enumerate(others)
    ]
    swap_sems = (swap_send, swap_recv)
    swaps = []
    swapped = ((shared_down, down_full), (turned_gate, gate_full), (turned_up, up_full))
    far_first = sorted(range(seq_count - 1), key=lambda i: abs(2 * (i + 1) - seq_count))
    rounds = [(which, i) for which in range(3) for i in far_first]

    def pump(point):
        for which, i in [rounds.pop(0) for _ in range(min(PLAN[point], len(rounds)))]:
            source, target = swapped[which]
            swaps.append(
                go(
                    Send(
                        source.at[unit_rows(others[i]), :],
                        target.at[:, own_depth],
                        swap_sems,
                        which * (seq_count - 1) + i,
                        (others[i], tp),
                    )
                )
            )

    def turn(raw, turned, full):
        for start in range(0, raw.shape[1], 128):
            turned[start : start + 128, :] = raw[:, start : start + 128].T
        full[:, own_depth] = turned[unit_rows(me), :]

    def relay(j):
        for way in range(2):
            for piece in range(2):
                hop[way, j - 1, piece].wait_recv()
                if j < groups - 1:
                    hop[way, j, piece] = go(kv_hop(way, j, piece))
                across[way, j, piece] = go(kv_across(way, j, piece))

    pump("sent")
    loads[4].wait()
    turn(raw_gate, turned_gate, gate_full)
    relay(1)
    pump("relay1")
    loads[5].wait()
    turn(raw_up, turned_up, up_full)
    for j in range(2, groups):
        relay(j)
        pump(f"relay{j}")

    for i in (0, 1, 2):
        loads[i].wait()
    for copy in note_copies:
        copy.wait_recv()
    own_segment = all_notes[me].T[:, 0:1]
    query_place = me * tokens + lax.broadcasted_iota(jnp.int32, (tokens, tokens), 0)
    for owner in range(seq_count):
        key_place = owner * tokens + lax.broadcasted_iota(jnp.int32, (tokens, tokens), 1)
        seen = (
            (own_segment == all_notes[owner, 0:1, :])
            & (key_place <= query_place)
            & ((all_notes[owner, 1:2, :] == 1) | (key_place == query_place))
        )
        bias[:, owner * tokens : (owner + 1) * tokens] = jnp.where(seen, 0.0, -jnp.inf)

    for copy in across.values():
        copy.wait_recv()
    pump("attend")
    for head in range(heads):
        cols = slice(head * HD, (head + 1) * HD)
        scores = nt(query_v[:, cols], kv[:, cols]) * HD**-0.5 + bias[...]
        raw = jnp.exp(scores - jnp.max(scores, 1, keepdims=True))
        total = jnp.sum(raw, 1, keepdims=True)
        values = kv[:, width + head * HD : width + (head + 1) * HD]
        mixed = jnp.dot(raw.astype(BF16), values, preferred_element_type=F32)
        attended[:, cols] = (mixed / total).astype(BF16)

    tp_sems = (tp_send, tp_recv)
    for i in (7, 8, 9):
        loads[i].wait()

    def part(owner):
        return jnp.dot(attended[...], out_weight_v[:, cols_of(owner)], preferred_element_type=F32)

    copies = []
    for k in (2, 1, 3):
        part_out[k - 1] = part(lax.rem(tp + k, 4)).astype(BF16)
        copies.append(
            go(Send(part_out.at[k - 1], part_in.at[k - 1], tp_sems, k - 1, row_peers[k - 1]))
        )
    pump("project")
    total = residual_v[...].astype(F32) + part(tp)
    for copy in copies:
        copy.wait_recv()
    for k in range(3):
        total += part_in[k].astype(F32)
    stream[...] = total
    mine[...] = (total * gain_v[...].astype(F32).reshape(1, width)).astype(BF16)

    row_sems = (row_send, row_recv)

    def row_view(owner, tp_owner):
        return rows.at[rows_of(owner), cols_of(tp_owner)]

    def row_hop(way, j, source=None):
        block = row_view(origin(way, j) * 2 + x, tp)
        return Send(
            block if source is None else source,
            block,
            row_sems,
            way * (groups - 1) + j,
            nexts[way],
            both(exists(way, j), beyond[way]),
            exists(way, j + 1),
        )

    def row_copy(kind, way, j, peer, other_x, other_y, source=None):
        owner = origin(way, j) * 2 + (1 - x if other_x else x)
        block = row_view(owner, lax.rem(tp + 2, 4) if other_y else tp)
        index = 2 * (groups - 1) + kind * count + slots.index((way, j))
        ok = exists(way, j)
        return go(Send(block if source is None else source, block, row_sems, index, peer, ok, ok))

    hop, across, over, diag, near = {}, {}, {}, {}, []

    def spread(way, j, source=None):
        across[way, j] = row_copy(0, way, j, pair, False, False, source)
        over[way, j] = row_copy(1, way, j, far, False, False, source)
        near.append(row_copy(3, way, j, core, False, False, source))

    for way in range(2):
        hop[way, 0] = go(row_hop(way, 0, mine))
    spread(0, 0, mine)
    place_mine = pltpu.make_async_copy(mine, row_view(me, tp), local.at[len(loads) + 1])
    place_mine.start()

    squares = jnp.sum(total * total, 1, keepdims=True)
    own_squares = jnp.broadcast_to(squares, (tokens, tokens)).T[0:8, :]
    square_out[0] = own_squares
    square_copies = [
        go(Send(square_out.at[0], square_in.at[k], tp_sems, 3 + k, row_peers[k])) for k in range(3)
    ]
    for copy in square_copies:
        copy.wait_recv()
    own_squares = own_squares + square_in[0] + square_in[1] + square_in[2]
    square_out[1] = own_squares
    square_all[me] = own_squares
    square_copies = [
        go(Send(square_out.at[1], square_all.at[me], tp_sems, 6 + i, (other, tp)))
        for i, other in enumerate(others)
    ]

    for j in range(1, groups):
        for way in range(2):
            hop[way, j - 1].wait_recv()
            if j < groups - 1:
                hop[way, j] = go(row_hop(way, j))
            spread(way, j)
        pump(f"rows{j}")
    for way, j in slots:
        pump("slot")
        across[way, j].wait_recv()
        near.append(row_copy(4, way, j, core, True, False))
        if j % 2 == 1:
            diag[way, j] = row_copy(2, way, j, far, True, False)
        over[way, j].wait_recv()
        near.append(row_copy(5, way, j, core, False, True))
        if j % 2 == 0:
            diag[way, j] = row_copy(2, way, j, pair, False, True)
    for way, j in slots:
        diag[way, j].wait_recv()
        near.append(row_copy(6, way, j, core, True, True))
    pump("rest")
    page_rows = kv_pages.shape[1]
    row = lax.broadcasted_iota(jnp.int32, (tokens, tokens), 0)
    col = lax.broadcasted_iota(jnp.int32, (tokens, tokens), 1)
    same_row = lax.rem(row, page_rows) == lax.rem(col, page_rows)
    wanted = me * pages.shape[0] + row // page_rows
    picks = [
        jnp.where(same_row & (all_notes[o, 2 + per_token : 3 + per_token, :] == wanted), 1.0, 0.0)
        for o in range(seq_count)
    ]
    picked = jnp.dot(
        jnp.concatenate(picks, 1).astype(BF16), kv[...], preferred_element_type=F32
    ).astype(BF16)
    for i in range(pages.shape[0]):
        kv_pages[i] = picked[i * page_rows : (i + 1) * page_rows, :]
    place_mine.wait()
    for copy in square_copies + near:
        copy.wait_recv()
    for i in (10, 11, 12, 13, 17):
        loads[i].wait()
    vector = jnp.broadcast_to(vector_v[...].astype(F32).reshape(1, D), (8, D))
    router_v[...] = jnp.concatenate([router_in[...].astype(F32), vector]).astype(BF16)

    red_sems = (red_send, red_recv)
    first_far, first_pair, first_down = 2 * groups, 4 * groups, 6 * groups
    lanes = lax.broadcasted_iota(jnp.int32, (tokens, 2 * seq_count), 1)

    def chunk(k):
        return pl.ds(pl.multiple_of(lax.rem(z + k, groups) * 2 * tokens, 2 * tokens), 2 * tokens)

    def scales(owner, logits, inverse):
        ids = all_notes[owner].T
        chosen = lanes == ids[:, 2:3]
        for k in range(1, per_token):
            chosen = chosen | (lanes == ids[:, 2 + k : 3 + k])
        logits = logits * inverse
        top = jnp.max(jnp.where(chosen, logits, -jnp.inf), 1, keepdims=True)
        raw = jnp.where(chosen, jnp.exp(logits - top), 0.0)
        route = jnp.sum(jnp.where(lanes == me, raw, 0.0), 1, keepdims=True) / jnp.sum(
            raw, 1, keepdims=True
        )
        share = jax.nn.sigmoid(logits[:, seq_count : seq_count + 1])
        return route, share

    factors = {}

    def hide(k, gates, ups, factor):
        block = rows[chunk(k), :]
        inverse = factors[k][0]
        return (
            jax.nn.silu(nt(block, gates) * inverse) * (nt(block, ups) * inverse) * factor
        ).astype(BF16)

    def fill(k):
        logits = nt(rows[chunk(k), :], router_v[...])
        first = lax.rem(z + k, groups) * 2
        found = []
        for i in range(2):
            squares = square_all[first + i].T[:, 0:1]
            inverse = lax.rsqrt(squares / D + norm_eps)
            found.append(
                (inverse,) + scales(first + i, logits[i * tokens : (i + 1) * tokens], inverse)
            )
        factors[k] = [jnp.concatenate(pieces, 0) for pieces in zip(*found)]
        hidden[chunk(k), :] = hide(k, gate_v[...], up_v[...], factors[k][1])

    def fill_shared(k):
        shared_hidden[chunk(k), :] = hide(k, gate_full[...], up_full[...], factors[k][2])

    def product(k, tp_owner):
        return jnp.dot(
            hidden[chunk(k), :], down_v[:, cols_of(tp_owner)], preferred_element_type=F32
        ) + jnp.dot(
            shared_hidden[chunk(k), :],
            down_full[:, cols_of(tp_owner)],
            preferred_element_type=F32,
        )

    order = list(range(1, groups)) + [0]
    for k in order:
        fill(k)
    loads[6].wait()
    for copy in swaps:
        copy.wait_recv()
    to_core, to_far, to_pair, far_more, pair_more, to_down = {}, {}, {}, {}, {}, []
    part = width // 2
    here, away = rows_of(x), rows_of(1 - x)

    def start_core(k):
        fill_shared(k)
        to_core[k] = []
        for side in range(2):
            core_out[k, side] = product(k, side * 2 + 1 - c).astype(BF16)
            to_core[k].append(
                go(
                    Send(
                        core_out.at[k, side], core_in.at[k, side], red_sems, 2 * k + side, core
                    )
                )
            )

    start_core(order[0])
    for step in range(groups + 2):
        if step + 1 < groups:
            start_core(order[step + 1])
        if step < groups:
            k = order[step]
            passed[k] = product(k, (1 - y) * 2 + c)
            kept[k] = product(k, tp)
            for copy in to_core[k]:
                copy.wait_recv()
            passed[k] = passed[k] + core_in[k, 1 - y].astype(F32)
            kept[k] = kept[k] + core_in[k, y].astype(F32)
            far_out[k] = passed[k, :, :part].astype(BF16)
            to_far[k] = go(Send(far_out.at[k], far_in.at[k], red_sems, first_far + 2 * k, far))
            pair_out[k, 0] = passed[k, away, part:].astype(BF16)
            pair_out[k, 1] = kept[k, away, part:].astype(BF16)
            to_pair[k] = go(
                Send(pair_out.at[k], pair_in.at[k], red_sems, first_pair + 2 * k, pair)
            )
        if 0 <= step - 1 < groups:
            k = order[step - 1]
            to_far[k].wait_recv()
            pair_more_out[k] = (
                kept[k, away, :part] + far_in[k, away, :].astype(F32)
            ).astype(BF16)
            pair_more[k] = go(
                Send(
                    pair_more_out.at[k], pair_more_in.at[k], red_sems, first_pair + 2 * k + 1, pair
                )
            )
            to_pair[k].wait_recv()
            far_more_out[k] = (passed[k, here, part:] + pair_in[k, 0].astype(F32)).astype(BF16)
            far_more[k] = go(
                Send(far_more_out.at[k], far_more_in.at[k], red_sems, first_far + 2 * k + 1, far)
            )
        if 0 <= step - 2 < groups:
            k = order[step - 2]
            pair_more[k].wait_recv()
            far_more[k].wait_recv()
            left = (
                kept[k, here, :part]
                + far_in[k, here, :].astype(F32)
                + pair_more_in[k].astype(F32)
            )
            right = (
                kept[k, here, part:] + pair_in[k, 1].astype(F32) + far_more_in[k].astype(F32)
            )
            if k == 0:
                half[:, :part] = left
                half[:, part:] = right
            else:
                down_out[k - 1, :, :part] = left.astype(BF16)
                down_out[k - 1, :, part:] = right.astype(BF16)
                to_down.append(
                    go(
                        Send(
                            down_out.at[k - 1],
                            down_in.at[k - 1],
                            red_sems,
                            first_down + k - 1,
                            column[k - 1],
                        )
                    )
                )
    for copy in to_down:
        copy.wait_recv()
    amount = half[...]
    for k in range(groups - 1):
        amount += down_in[k].astype(F32)
    out[...] = amount
    for copy in sent:
        copy.wait_send()


def whole_layer(
    query,
    key,
    value,
    segments,
    pads,
    choices,
    pages,
    shared_gate,
    shared_up,
    shared_down,
    out_weight,
    residual,
    gain,
    router,
    shared_vector,
    gate,
    up,
    down,
):
    seq_count = lax.axis_size("seq")
    groups = seq_count // 2
    tokens, width = query.shape
    depth, all_units = shared_gate.shape
    units = all_units // seq_count
    total, features = seq_count * tokens, 4 * width
    count = 2 * groups - 1
    hops = 2 * (groups - 1)
    per_token, page_count = choices.shape[0], pages.shape[0]

    def vmem(*shape, dtype=BF16):
        return pltpu.VMEM(shape, dtype)

    def sems(number):
        return [pltpu.SemaphoreType.DMA((number,))] * 2

    block = jax.ShapeDtypeStruct((tokens, width), F32)
    return pl.pallas_call(
        functools.partial(layer_kernel, seq_count, per_token),
        out_shape=(
            block,
            block,
            jax.ShapeDtypeStruct((page_count, tokens // page_count, 2 * width), BF16),
        ),
        in_specs=[pl.BlockSpec(memory_space=pl.ANY)] * 18,
        out_specs=[pl.BlockSpec(memory_space=pltpu.VMEM)] * 3,
        scratch_shapes=[
            vmem(seq_count, 8, tokens, dtype=jnp.int32),
            vmem(tokens, dtype=jnp.int32),
            vmem(tokens, dtype=jnp.int32),
            vmem(per_token, tokens, dtype=jnp.int32),
            pltpu.SMEM((page_count,), jnp.int32),
            vmem(tokens, width),
            vmem(total, 2 * width),
            vmem(depth, all_units),
            vmem(depth, all_units),
            vmem(all_units, depth),
            vmem(all_units, depth),
            vmem(units, features),
            vmem(units, features),
            vmem(units, features),
            vmem(*out_weight.shape),
            vmem(tokens, width),
            vmem(width),
            vmem(*router.shape),
            vmem(*shared_vector.shape),
            vmem(2 * seq_count, features),
            vmem(*gate.shape),
            vmem(*up.shape),
            vmem(*down.shape),
            vmem(tokens, total, dtype=F32),
            vmem(tokens, width),
            vmem(3, tokens, width),
            vmem(3, tokens, width),
            vmem(2, 8, tokens, dtype=F32),
            vmem(3, 8, tokens, dtype=F32),
            vmem(seq_count, 8, tokens, dtype=F32),
            vmem(tokens, width),
            vmem(total, features),
            vmem(total, gate.shape[0]),
            vmem(total, units),
            vmem(groups, 2, 2 * tokens, width),
            vmem(groups, 2, 2 * tokens, width),
            vmem(groups, 2 * tokens, width // 2),
            vmem(groups, 2 * tokens, width // 2),
            vmem(groups, 2, tokens, width // 2),
            vmem(groups, 2, tokens, width // 2),
            vmem(groups, tokens, width // 2),
            vmem(groups, tokens, width // 2),
            vmem(groups, tokens, width // 2),
            vmem(groups, tokens, width // 2),
            vmem(groups - 1, tokens, width),
            vmem(groups - 1, tokens, width),
            vmem(groups, 2 * tokens, width, dtype=F32),
            vmem(groups, 2 * tokens, width, dtype=F32),
            vmem(tokens, width, dtype=F32),
            pltpu.SemaphoreType.DMA((24,)),
        ]
        + sems(2 * (hops + count))
        + sems(seq_count - 1)
        + sems(3 * (seq_count - 1))
        + sems(6 + seq_count - 1)
        + sems(hops + 7 * count)
        + sems(7 * groups - 1),
        compiler_params=pltpu.CompilerParams(
            collective_id=0, has_side_effects=True, vmem_limit_bytes=56 * 2**20
        ),
        cost_estimate=pl.CostEstimate(
            flops=8_000_000_000, transcendentals=1_000_000, bytes_accessed=30_000_000
        ),
    )(
        query,
        key,
        value,
        segments,
        pads,
        choices,
        pages,
        shared_gate,
        shared_up,
        shared_down,
        out_weight,
        residual,
        gain,
        router,
        shared_vector,
        gate,
        up,
        down,
    )


def head_scores(query_heads, key_heads):
    score_scale = query_heads.shape[-1] ** (-0.5)
    return (
        jnp.einsum("qhd,khd->hqk", query_heads, key_heads, preferred_element_type=jnp.float32)
        * score_scale
    )


def run_experts(rows_in, gate_weight, up_weight, down_weight):
    local_experts = gate_weight.shape[0]
    sources = rows_in.shape[0] // local_experts
    grouped = rows_in.reshape(sources, local_experts, rows_in.shape[1], rows_in.shape[2])
    gate_act = jnp.einsum(
        "nesd,edf->nesf", grouped, gate_weight, preferred_element_type=jnp.float32
    )
    up_act = jnp.einsum("nesd,edf->nesf", grouped, up_weight, preferred_element_type=jnp.float32)
    hidden = (jax.nn.silu(gate_act) * up_act).astype(jnp.bfloat16)
    partial_out = jnp.einsum(
        "nesf,efd->nesd", hidden, down_weight, preferred_element_type=jnp.float32
    )
    partial_out = partial_out.reshape(rows_in.shape[0], rows_in.shape[1], down_weight.shape[2])
    summed = lax.psum_scatter(
        partial_out.astype(jnp.bfloat16), "tp", scatter_dimension=2, tiled=True
    )
    return lax.all_to_all(summed, "seq", split_axis=0, concat_axis=0, tiled=True)


def per_device(
    query_rows,
    key_rows,
    value_rows,
    residual,
    out_weight,
    norm_gain,
    router_weight,
    expert_ids,
    gate_weight,
    up_weight,
    down_weight,
    shared_gate_weight,
    shared_up_weight,
    shared_down_weight,
    shared_gate_vector,
    segment_ids,
    pad_mask,
    page_table,
):
    tokens_here = query_rows.shape[0]
    feat_width = query_rows.shape[1]
    heads_here = feat_width // HD
    seq_count = lax.axis_size("seq")
    me = lax.axis_index("seq")
    expert_count = seq_count * gate_weight.shape[0]
    per_token = expert_ids.shape[1]
    pages_here = page_table.shape[0]
    page_rows = tokens_here // pages_here
    capacity = 2 * tokens_here * per_token // expert_count
    query_heads = query_rows.reshape(tokens_here, heads_here, HD)
    dense = (
        capacity >= tokens_here
        and gate_weight.shape[0] == 1
        and seq_count % 2 == 0
        and lax.axis_size("tp") == 4
        and per_token <= 5
        and seq_count == 8
    )
    if dense:
        stream, mixture, kv_cache = whole_layer(
            query_rows,
            key_rows,
            value_rows,
            segment_ids,
            pad_mask,
            expert_ids.T,
            page_table,
            shared_gate_weight,
            shared_up_weight,
            shared_down_weight,
            out_weight,
            residual,
            norm_gain,
            router_weight.T,
            shared_gate_vector,
            gate_weight[0].T,
            up_weight[0].T,
            down_weight[0],
        )
        return stream + mixture, kv_cache
    kv_local = jnp.concatenate([key_rows, value_rows], 1)
    notes = jnp.concatenate([segment_ids, pad_mask, expert_ids.T.reshape(-1), page_table])
    all_notes = lax.all_gather(notes, "seq", axis=0, tiled=False)
    gathered_kv = lax.all_gather(kv_local, "seq", axis=0, tiled=True)
    window = min(seq_count, REACH + 1)
    first = jnp.clip(me - REACH, 0, seq_count - window)
    if window == seq_count:
        all_kv, window_notes = gathered_kv, all_notes
    else:
        all_kv = lax.dynamic_slice_in_dim(gathered_kv, first * tokens_here, window * tokens_here, 0)
        window_notes = lax.dynamic_slice_in_dim(all_notes, first, window, 0)
    key_segment = window_notes[:, :tokens_here].reshape(-1)
    key_mask = window_notes[:, tokens_here : 2 * tokens_here].reshape(-1)
    query_place = (me - first) * tokens_here + jnp.arange(tokens_here, dtype=jnp.int32)
    key_place = jnp.arange(window * tokens_here, dtype=jnp.int32)
    all_visible = (
        (segment_ids[:, None] == key_segment[None, :])
        & (key_place[None, :] <= query_place[:, None])
        & ((key_mask[None, :] == 1) | (key_place[None, :] == query_place[:, None]))
    )
    key_heads = all_kv[:, :feat_width].reshape(-1, heads_here, HD)
    scores = jnp.where(all_visible[None], head_scores(query_heads, key_heads), -jnp.inf)
    row_top = jnp.max(scores, -1)
    weights_raw = jnp.exp(scores - row_top[..., None])
    row_total = jnp.sum(weights_raw, -1)
    all_values = all_kv[:, feat_width:].reshape(-1, heads_here, HD)
    mixed_heads = jnp.einsum(
        "hqk,khd->qhd",
        weights_raw.astype(jnp.bfloat16),
        all_values,
        preferred_element_type=jnp.float32,
    )
    all_slots = all_notes[:, -pages_here:].reshape(-1)
    my_slots = me * pages_here + jnp.arange(pages_here, dtype=jnp.int32)
    my_pages = jnp.argmax(all_slots[None, :] == my_slots[:, None], 1)
    kv_cache = jnp.stack(
        [
            lax.dynamic_slice_in_dim(gathered_kv, my_pages[page] * page_rows, page_rows, 0)
            for page in range(pages_here)
        ]
    )
    attended = (
        (mixed_heads / row_total.T[:, :, None])
        .astype(jnp.bfloat16)
        .reshape(tokens_here, feat_width)
    )
    projected = jnp.dot(attended, out_weight, preferred_element_type=jnp.float32)
    projected = lax.psum_scatter(
        projected.astype(jnp.bfloat16), "tp", scatter_dimension=1, tiled=True
    ).astype(jnp.float32)
    stream = residual.astype(jnp.float32) + projected
    square_sum = lax.psum(jnp.sum(stream * stream, 1), "tp")
    normed = (
        stream * lax.rsqrt(square_sum / D + norm_eps)[:, None] * norm_gain.astype(jnp.float32)
    ).astype(jnp.bfloat16)
    full_normed = lax.all_gather(normed, "tp", axis=1, tiled=True)
    logits = jnp.dot(full_normed, router_weight, preferred_element_type=jnp.float32)
    shared_gate_act = jnp.dot(
        full_normed,
        lax.all_gather(shared_gate_weight, "seq", axis=0, tiled=True),
        preferred_element_type=jnp.float32,
    )
    shared_up_act = jnp.dot(
        full_normed,
        lax.all_gather(shared_up_weight, "seq", axis=0, tiled=True),
        preferred_element_type=jnp.float32,
    )
    shared_hidden = (jax.nn.silu(shared_gate_act) * shared_up_act).astype(jnp.bfloat16)
    shared_part = jnp.dot(
        shared_hidden,
        lax.all_gather(shared_down_weight, "seq", axis=1, tiled=True),
        preferred_element_type=jnp.float32,
    )
    shared_out = lax.psum_scatter(
        shared_part.astype(jnp.bfloat16), "tp", scatter_dimension=1, tiled=True
    ).astype(jnp.float32)
    shared_scale = jax.nn.sigmoid(
        jnp.dot(full_normed, shared_gate_vector, preferred_element_type=jnp.float32)
    )
    flat_expert = expert_ids.reshape(-1)
    expert_range = jnp.arange(expert_count, dtype=jnp.int32)
    onehot = (flat_expert[:, None] == expert_range[None, :]).astype(BF16)
    place_range = jnp.arange(flat_expert.shape[0], dtype=jnp.int32)
    earlier = (place_range[:, None] >= place_range[None, :]).astype(BF16)
    running = jnp.dot(earlier, onehot, preferred_element_type=F32)
    slot_rank = jnp.sum(running * onehot.astype(F32), 1).astype(jnp.int32) - 1
    slot_index = flat_expert * capacity + slot_rank
    token_of = jnp.arange(tokens_here * per_token, dtype=jnp.int32) // per_token
    source_row = (
        jnp.full((expert_count * capacity,), tokens_here, jnp.int32).at[slot_index].set(token_of)
    )
    slice_width = normed.shape[1]
    padded_rows = jnp.concatenate([normed, jnp.zeros((1, slice_width), jnp.bfloat16)], 0)
    outgoing = padded_rows[source_row].reshape(expert_count, capacity, slice_width)
    whole_rows = lax.all_gather(
        lax.all_to_all(outgoing, "seq", split_axis=0, concat_axis=0, tiled=True),
        "tp",
        axis=2,
        tiled=True,
    )
    returned = run_experts(whole_rows, gate_weight, up_weight, down_weight)
    chosen = expert_ids[:, :, None] == expert_range[None, None, :]
    chosen_logits = jnp.sum(jnp.where(chosen, logits[:, None, :], 0.0), 2)
    choice_top = jnp.max(chosen_logits, 1, keepdims=True)
    choice_exp = jnp.exp(chosen_logits - choice_top)
    route_weight = choice_exp / jnp.sum(choice_exp, 1, keepdims=True)
    back_rows = returned.reshape(expert_count * capacity, returned.shape[2])[slot_index]
    weighted = (
        back_rows.astype(jnp.float32).reshape(tokens_here, per_token, returned.shape[2])
        * route_weight[:, :, None]
    )
    layer_out = stream + jnp.sum(weighted, 1) + shared_scale[:, None] * shared_out
    return (layer_out, kv_cache)


def solution(mesh):
    placed = (
        P("seq", "tp"),
        P("seq", "tp"),
        P("seq", "tp"),
        P("seq", "tp"),
        P("tp", None),
        P("tp"),
        P(),
        P("seq", None),
        P("seq", None, "tp"),
        P("seq", None, "tp"),
        P("seq", "tp", None),
        P("seq", "tp"),
        P("seq", "tp"),
        P("tp", "seq"),
        P(),
        P("seq"),
        P("seq"),
        P("seq"),
    )
    return jax.shard_map(
        per_device,
        mesh=mesh,
        in_specs=placed,
        out_specs=(P("seq", "tp"), P("seq", None, "tp")),
        check_vma=False,
    )
```

```python
import functools

import jax
import jax.numpy as jnp
from jax import lax
from jax.experimental import pallas as pl
from jax.experimental.pallas import tpu as pltpu
from jax.sharding import PartitionSpec as P

D = 2048
HD = 128
REACH = 7


norm_eps = 1e-06


MESH = pl.DeviceIdType.MESH
BF16, F32 = jnp.bfloat16, jnp.float32


BY_Y = (1, 3)
DOWN, GATE, UP = range(3)
PLAN = {
    "attend": [
        (1, 2, DOWN),
        (1, 2, GATE),
        (1, 2, UP),
        (0, 1, DOWN),
        (0, 1, GATE),
        (0, 1, UP),
        (2, 3, DOWN),
        (2, 3, GATE),
        (2, 3, UP),
    ],
    "rows3": [
        (0, 3, DOWN),
        (0, 3, GATE),
        (0, 3, UP),
        (1, 3, DOWN),
        (1, 3, GATE),
        (1, 3, UP),
        (0, 2, DOWN),
        (0, 2, GATE),
        (0, 2, UP),
        (0, 0, DOWN),
        (0, 0, GATE),
        (0, 0, UP),
    ],
}


def place(seq_count):
    me, tp = lax.axis_index("seq"), lax.axis_index("tp")
    return me, tp, me // 2, lax.rem(me, 2), seq_count // 2


def greet(peers):
    barrier = pltpu.get_barrier_semaphore()
    for peer in peers:
        pl.semaphore_signal(barrier, inc=1, device_id=peer, device_id_type=MESH)
    pl.semaphore_wait(barrier, len(peers))


def remote(src, dst, sems, index, peer):
    copy = pltpu.make_async_remote_copy(
        src_ref=src,
        dst_ref=dst,
        send_sem=sems[0].at[index],
        recv_sem=sems[1].at[index],
        device_id=peer,
        device_id_type=MESH,
    )
    copy.start()
    return copy


def nt(left, right):
    return lax.dot_general(left, right, (((1,), (1,)), ((), ())), preferred_element_type=F32)


def maybe(condition, action):
    if condition is None:
        action()
    else:
        pl.when(condition)(action)


class Send:
    def __init__(self, src, dst, sems, index, peer, go=None, come=None):
        self.go, self.come = go, come
        self.make = lambda: pltpu.make_async_remote_copy(
            src_ref=src,
            dst_ref=dst,
            send_sem=sems[0].at[index],
            recv_sem=sems[1].at[index],
            device_id=peer,
            device_id_type=MESH,
        )

    left = False

    def start(self):
        maybe(self.go, lambda: self.make().start())
        return self

    def wait_recv(self):
        maybe(self.come, lambda: self.make().wait_recv())

    def wait_send(self):
        if not self.left:
            maybe(self.go, lambda: self.make().wait_send())
        self.left = True


def both(first, second):
    if first is None:
        return second
    if second is None:
        return first
    return jnp.logical_and(first, second)


def layer_kernel(
    seq_count,
    per_token,
    query,
    key,
    value,
    segments,
    pads,
    choices,
    pages,
    shared_gate,
    shared_up,
    shared_down,
    out_weight,
    residual,
    gain,
    router,
    shared_vector,
    gate,
    up,
    down,
    stream,
    out,
    kv_pages,
    all_notes,
    segments_v,
    pads_v,
    choices_v,
    pages_s,
    query_v,
    kv,
    raw_gate,
    raw_up,
    turned_gate,
    turned_up,
    gate_full,
    up_full,
    down_full,
    out_weight_v,
    residual_v,
    gain_v,
    router_in,
    vector_v,
    router_v,
    gate_v,
    up_v,
    down_v,
    bias,
    both_attended,
    attended,
    page_out,
    page_in,
    part_out,
    part_in,
    square_out,
    square_in,
    square_all,
    mine,
    rows,
    hidden,
    shared_hidden,
    core_out,
    core_in,
    far_out,
    far_in,
    pair_out,
    pair_in,
    far_more_out,
    far_more_in,
    pair_more_out,
    pair_more_in,
    down_out,
    down_in,
    kept,
    passed,
    half,
    local,
    kv_send,
    kv_recv,
    note_send,
    note_recv,
    swap_send,
    swap_recv,
    tp_send,
    tp_recv,
    row_send,
    row_recv,
    red_send,
    red_recv,
):
    me, tp, z, x, groups = place(seq_count)
    tokens, width = query.shape
    depth = shared_gate.shape[0]
    units = shared_gate.shape[1] // seq_count
    heads = width // HD
    y, c = tp // 2, lax.rem(tp, 2)
    others = [lax.rem(me + k, seq_count) for k in range(1, seq_count)]
    row_peers = [(me, lax.rem(tp + k, 4)) for k in range(1, 4)]
    pair = (z * 2 + 1 - x, tp)
    core = (me, y * 2 + 1 - c)
    far = (me, lax.rem(tp + 2, 4))
    column = [(lax.rem(z + k, groups) * 2 + x, tp) for k in range(1, groups)]
    nexts = [(lax.rem(z + 1, groups) * 2 + x, tp), (lax.rem(z + groups - 1, groups) * 2 + x, tp)]
    beyond = [z + 1 < groups, z >= 1]
    slots = [(0, 0)] + [(way, j) for j in range(1, groups) for way in range(2)]
    count = len(slots)
    sent = []

    def exists(way, j):
        if j == 0:
            return None
        return z >= j if way == 0 else z + j < groups

    def origin(way, j):
        return lax.rem(z + groups - j, groups) if way == 0 else lax.rem(z + j, groups)

    def rows_of(owner):
        return pl.ds(pl.multiple_of(owner * tokens, tokens), tokens)

    def cols_of(tp_owner):
        return pl.ds(pl.multiple_of(tp_owner * width, width), width)

    own_depth = pl.ds(pl.multiple_of(me * depth, depth), depth)

    def unit_rows(owner):
        return pl.ds(pl.multiple_of(owner * units, units), units)

    part = width // 2

    def half_cols(side):
        return pl.ds(pl.multiple_of(side * part, part), part)

    own_key = kv.at[rows_of(me), pl.ds(0, part)]
    own_value = kv.at[rows_of(me), pl.ds(part, part)]
    loads = [
        (query.at[:, half_cols(x)], query_v.at[x]),
        (key.at[:, half_cols(x)], own_key),
        (value.at[:, half_cols(x)], own_value),
        (segments, segments_v),
        (shared_gate, raw_gate),
        (shared_up, raw_up),
        (shared_down.at[unit_rows(me), :], down_full.at[:, own_depth]),
        (out_weight, out_weight_v),
        (residual, residual_v),
        (gain, gain_v),
        (router, router_in),
        (gate, gate_v),
        (up, up_v),
        (down, down_v),
        (pads, pads_v),
        (choices, choices_v),
        (pages, pages_s),
        (shared_vector, vector_v),
    ]
    loads = [pltpu.make_async_copy(a, b, local.at[i]) for i, (a, b) in enumerate(loads)]
    for copy in loads:
        copy.start()
    greet([(other, tp) for other in others] + row_peers)

    kv_sems = (kv_send, kv_recv)
    first_cross = 4 * (groups - 1)

    def kv_hop(way, j, piece):
        block = kv.at[rows_of(origin(way, j) * 2 + (x if piece == 0 else 1 - x)), :]
        return Send(
            block,
            block,
            kv_sems,
            (piece * 2 + way) * (groups - 1) + j,
            nexts[way],
            both(exists(way, j), beyond[way]),
            exists(way, j + 1),
        )

    def go(copy):
        sent.append(copy.start())
        return copy

    hop = {}
    crossed = [
        go(Send(source.at[:, half_cols(1 - x)], target, kv_sems, first_cross + i, pair))
        for i, (source, target) in enumerate(
            ((key, own_key), (value, own_value), (query, query_v.at[x]))
        )
    ]
    loads[1].wait()
    loads[2].wait()
    for way in range(2):
        hop[way, 0, 0] = go(kv_hop(way, 0, 0))
    note_sems = (note_send, note_recv)
    for i in (3, 14, 15, 16):
        loads[i].wait()
    page_lane = lax.broadcasted_iota(jnp.int32, (1, tokens), 1)
    page_row = jnp.zeros((1, tokens), jnp.int32)
    for i in range(pages.shape[0]):
        page_row = jnp.where(page_lane // kv_pages.shape[1] == i, pages_s[i], page_row)
    all_notes[me] = jnp.concatenate(
        [
            segments_v[...].reshape(1, tokens),
            pads_v[...].reshape(1, tokens),
            choices_v[...],
            page_row,
            jnp.zeros((5 - per_token, tokens), jnp.int32),
        ]
    )
    note_copies = [
        go(Send(all_notes.at[me], all_notes.at[me], note_sems, i, (other, tp)))
        for i, other in enumerate(others)
    ]
    swap_sems = (swap_send, swap_recv)
    swapped = ((shared_down, down_full), (turned_gate, gate_full), (turned_up, up_full))
    def goes(a, b, i):
        to_z = others[i] // 2
        if a == b:
            return to_z == z
        up_way = jnp.logical_and(z == a, to_z == b)
        return jnp.logical_or(
            up_way, jnp.logical_and(z == groups - 1 - a, to_z == groups - 1 - b)
        )

    def may_go(a, b, i):
        steps = {(i + 1) // 2 % groups, (i + 2) // 2 % groups}
        return bool(steps & {b - a, (a - b) % groups})

    def swap(which, i, go_if):
        source, target = swapped[which]
        return Send(
            source.at[unit_rows(others[i]), :],
            target.at[:, own_depth],
            swap_sems,
            which * (seq_count - 1) + i,
            (others[i], tp),
            go_if,
        )

    def pump(point):
        for a, b, which in PLAN.get(point, ()):
            for i in range(seq_count - 1):
                if may_go(a, b, i):
                    swap(which, i, goes(a, b, i)).start()

    def turn(raw, turned, full):
        for start in range(0, raw.shape[1], 128):
            turned[start : start + 128, :] = raw[:, start : start + 128].T
        full[:, own_depth] = turned[unit_rows(me), :]

    def relay(j):
        for piece in range(2):
            for way in range(2):
                hop[way, j - 1, piece].wait_recv()
                if j < groups - 1:
                    hop[way, j, piece] = go(kv_hop(way, j, piece))

    crossed[0].wait_recv()
    crossed[1].wait_recv()
    for way in range(2):
        hop[way, 0, 1] = go(kv_hop(way, 0, 1))
    pump("sent")
    loads[4].wait()
    turn(raw_gate, turned_gate, gate_full)
    pump("turned1")
    loads[5].wait()
    turn(raw_up, turned_up, up_full)
    pump("turned2")
    relay(1)
    for way in range(2):
        for piece in range(2):
            hop[way, 1, piece].wait_send()
    pump("relay1")
    for j in range(2, groups):
        relay(j)
        pump(f"relay{j}")

    loads[0].wait()
    for copy in note_copies:
        copy.wait_recv()
    own_segment = jnp.concatenate([all_notes[z * 2 + side].T[:, 0:1] for side in range(2)], 0)
    query_place = z * 2 * tokens + lax.broadcasted_iota(jnp.int32, (2 * tokens, tokens), 0)
    for owner in range(seq_count):
        key_place = owner * tokens + lax.broadcasted_iota(jnp.int32, (2 * tokens, tokens), 1)
        seen = (
            (own_segment == all_notes[owner, 0:1, :])
            & (key_place <= query_place)
            & ((all_notes[owner, 1:2, :] == 1) | (key_place == query_place))
        )
        bias[:, owner * tokens : (owner + 1) * tokens] = jnp.where(seen, 0.0, -jnp.inf)

    crossed[2].wait_recv()
    pump("attend")
    for head in range(heads // 2):
        cols = slice(head * HD, (head + 1) * HD)
        queries = query_v[:, :, cols].reshape(2 * tokens, HD)
        scores = nt(queries, kv[:, cols]) * HD**-0.5 + bias[...]
        raw = jnp.exp(scores - jnp.max(scores, 1, keepdims=True))
        total = jnp.sum(raw, 1, keepdims=True)
        values = kv[:, part + head * HD : part + (head + 1) * HD]
        mixed = jnp.dot(raw.astype(BF16), values, preferred_element_type=F32)
        mixed = (mixed / total).astype(BF16)
        both_attended[:, :, cols] = mixed.reshape(2, tokens, HD)
    attended_back = go(
        Send(
            both_attended.at[1 - x],
            attended.at[:, half_cols(x)],
            kv_sems,
            first_cross + 3,
            pair,
        )
    )
    attended[:, half_cols(x)] = both_attended[x]
    for i in (7, 8, 9):
        loads[i].wait()
    attended_back.wait_recv()

    tp_sems = (tp_send, tp_recv)

    def project(owner):
        return jnp.dot(attended[...], out_weight_v[:, cols_of(owner)], preferred_element_type=F32)

    copies = []
    for k in (2, 1, 3):
        part_out[k - 1] = project(lax.rem(tp + k, 4)).astype(BF16)
        copies.append(
            go(Send(part_out.at[k - 1], part_in.at[k - 1], tp_sems, k - 1, row_peers[k - 1]))
        )
    pump("project")
    total = residual_v[...].astype(F32) + project(tp)
    for copy in copies:
        copy.wait_recv()
    for k in range(3):
        total += part_in[k].astype(F32)
    stream[...] = total
    mine[...] = (total * gain_v[...].astype(F32).reshape(1, width)).astype(BF16)

    row_sems = (row_send, row_recv)

    def row_view(owner, tp_owner):
        return rows.at[rows_of(owner), cols_of(tp_owner)]

    def row_hop(way, j):
        to_z = lax.rem(z + (j if way == 0 else groups - j), groups)
        return Send(
            mine,
            row_view(me, tp),
            row_sems,
            way * (groups - 1) + j - 1,
            (to_z * 2 + x, tp),
            z + j < groups if way == 0 else z >= j,
            exists(way, j),
        )

    def row_copy(kind, way, j, peer, other_x, other_y, source=None):
        owner = origin(way, j) * 2 + (1 - x if other_x else x)
        block = row_view(owner, lax.rem(tp + 2, 4) if other_y else tp)
        index = 2 * (groups - 1) + kind * count + slots.index((way, j))
        ok = exists(way, j)
        return go(Send(block if source is None else source, block, row_sems, index, peer, ok, ok))

    hop, across, over, diag, near = {}, {}, {}, {}, []

    def spread(way, j, source=None):
        across[way, j] = row_copy(0, way, j, pair, False, False, source)
        over[way, j] = row_copy(1, way, j, far, False, False, source)
        near.append(row_copy(3, way, j, core, False, False, source))

    for j in range(1, groups):
        for way in range(2):
            hop[way, j] = go(row_hop(way, j))
    spread(0, 0, mine)
    pump("rows")
    place_mine = pltpu.make_async_copy(mine, row_view(me, tp), local.at[len(loads) + 1])
    place_mine.start()

    squares = jnp.sum(total * total, 1, keepdims=True)
    own_squares = jnp.broadcast_to(squares, (tokens, tokens)).T[0:8, :]
    square_out[0] = own_squares
    square_copies = [
        go(Send(square_out.at[0], square_in.at[k], tp_sems, 3 + k, row_peers[k])) for k in range(3)
    ]
    for copy in square_copies:
        copy.wait_recv()
    own_squares = own_squares + square_in[0] + square_in[1] + square_in[2]
    square_out[1] = own_squares
    square_all[me] = own_squares
    square_copies = [
        go(Send(square_out.at[1], square_all.at[me], tp_sems, 6 + i, (other, tp)))
        for i, other in enumerate(others)
    ]

    for j in range(1, groups):
        for way in range(2):
            hop[way, j].wait_recv()
            spread(way, j)
        pump(f"rows{j}")
    for way, j in slots:
        pump("slot")
        across[way, j].wait_recv()
        near.append(row_copy(4, way, j, core, True, False))
        if j in BY_Y:
            diag[way, j] = row_copy(2, way, j, far, True, False)
        over[way, j].wait_recv()
        near.append(row_copy(5, way, j, core, False, True))
        if j not in BY_Y:
            diag[way, j] = row_copy(2, way, j, pair, False, True)
    for way, j in slots:
        diag[way, j].wait_recv()
        near.append(row_copy(6, way, j, core, True, True))
    pump("rest")
    page_rows = kv_pages.shape[1]
    row = lax.broadcasted_iota(jnp.int32, (2 * tokens, tokens), 0)
    col = lax.broadcasted_iota(jnp.int32, (2 * tokens, tokens), 1)
    same_row = lax.rem(row, page_rows) == lax.rem(col, page_rows)
    wanted = z * 2 * pages.shape[0] + row // page_rows
    picks = [
        jnp.where(same_row & (all_notes[o, 2 + per_token : 3 + per_token, :] == wanted), 1.0, 0.0)
        for o in range(seq_count)
    ]
    picked = jnp.dot(
        jnp.concatenate(picks, 1).astype(BF16), kv[...], preferred_element_type=F32
    ).astype(BF16)
    page_out[...] = picked.reshape(2, tokens, width)
    page_copy = go(Send(page_out.at[1 - x], page_in, kv_sems, first_cross + 4, pair))
    place_mine.wait()
    for copy in square_copies + near:
        copy.wait_recv()
    for i in (10, 11, 12, 13, 17):
        loads[i].wait()
    vector = jnp.broadcast_to(vector_v[...].astype(F32).reshape(1, D), (8, D))
    router_v[...] = jnp.concatenate([router_in[...].astype(F32), vector]).astype(BF16)

    red_sems = (red_send, red_recv)
    first_far, first_pair, first_down = 2 * groups, 4 * groups, 6 * groups
    lanes = lax.broadcasted_iota(jnp.int32, (tokens, 2 * seq_count), 1)

    def chunk(k):
        return pl.ds(pl.multiple_of(lax.rem(z + k, groups) * 2 * tokens, 2 * tokens), 2 * tokens)

    def scales(owner, logits, inverse):
        ids = all_notes[owner].T
        chosen = lanes == ids[:, 2:3]
        for k in range(1, per_token):
            chosen = chosen | (lanes == ids[:, 2 + k : 3 + k])
        logits = logits * inverse
        top = jnp.max(jnp.where(chosen, logits, -jnp.inf), 1, keepdims=True)
        raw = jnp.where(chosen, jnp.exp(logits - top), 0.0)
        route = jnp.sum(jnp.where(lanes == me, raw, 0.0), 1, keepdims=True) / jnp.sum(
            raw, 1, keepdims=True
        )
        share = jax.nn.sigmoid(logits[:, seq_count : seq_count + 1])
        return route, share

    factors = {}

    def hide(k, gates, ups, factor):
        block = rows[chunk(k), :]
        inverse = factors[k][0]
        return (
            jax.nn.silu(nt(block, gates) * inverse) * (nt(block, ups) * inverse) * factor
        ).astype(BF16)

    def fill(k):
        logits = nt(rows[chunk(k), :], router_v[...])
        first = lax.rem(z + k, groups) * 2
        found = []
        for i in range(2):
            squares = square_all[first + i].T[:, 0:1]
            inverse = lax.rsqrt(squares / D + norm_eps)
            found.append(
                (inverse,) + scales(first + i, logits[i * tokens : (i + 1) * tokens], inverse)
            )
        factors[k] = [jnp.concatenate(pieces, 0) for pieces in zip(*found)]
        hidden[chunk(k), :] = hide(k, gate_v[...], up_v[...], factors[k][1])

    def fill_shared(k):
        shared_hidden[chunk(k), :] = hide(k, gate_full[...], up_full[...], factors[k][2])

    def product(k, tp_owner):
        return jnp.dot(
            hidden[chunk(k), :], down_v[:, cols_of(tp_owner)], preferred_element_type=F32
        ) + jnp.dot(
            shared_hidden[chunk(k), :],
            down_full[:, cols_of(tp_owner)],
            preferred_element_type=F32,
        )

    order = list(range(1, groups)) + [0]
    for k in order:
        fill(k)
    loads[6].wait()
    swaps = [swap(which, i, None) for which in range(3) for i in range(seq_count - 1)]
    for copy in swaps:
        copy.wait_recv()
    to_core, to_far, to_pair, far_more, pair_more, to_down = {}, {}, {}, {}, {}, []
    here, away = rows_of(x), rows_of(1 - x)

    def start_core(k):
        fill_shared(k)
        to_core[k] = []
        for side in range(2):
            core_out[k, side] = product(k, side * 2 + 1 - c).astype(BF16)
            to_core[k].append(
                go(
                    Send(
                        core_out.at[k, side], core_in.at[k, side], red_sems, 2 * k + side, core
                    )
                )
            )

    start_core(order[0])
    for step in range(groups + 2):
        if step + 1 < groups:
            start_core(order[step + 1])
        if step < groups:
            k = order[step]
            passed[k] = product(k, (1 - y) * 2 + c)
            kept[k] = product(k, tp)
            for copy in to_core[k]:
                copy.wait_recv()
            passed[k] = passed[k] + core_in[k, 1 - y].astype(F32)
            kept[k] = kept[k] + core_in[k, y].astype(F32)
            far_out[k] = passed[k, :, :part].astype(BF16)
            to_far[k] = go(Send(far_out.at[k], far_in.at[k], red_sems, first_far + 2 * k, far))
            pair_out[k, 0] = passed[k, away, part:].astype(BF16)
            pair_out[k, 1] = kept[k, away, part:].astype(BF16)
            to_pair[k] = go(
                Send(pair_out.at[k], pair_in.at[k], red_sems, first_pair + 2 * k, pair)
            )
        if 0 <= step - 1 < groups:
            k = order[step - 1]
            to_far[k].wait_recv()
            pair_more_out[k] = (
                kept[k, away, :part] + far_in[k, away, :].astype(F32)
            ).astype(BF16)
            pair_more[k] = go(
                Send(
                    pair_more_out.at[k], pair_more_in.at[k], red_sems, first_pair + 2 * k + 1, pair
                )
            )
            to_pair[k].wait_recv()
            far_more_out[k] = (passed[k, here, part:] + pair_in[k, 0].astype(F32)).astype(BF16)
            far_more[k] = go(
                Send(far_more_out.at[k], far_more_in.at[k], red_sems, first_far + 2 * k + 1, far)
            )
        if 0 <= step - 2 < groups:
            k = order[step - 2]
            pair_more[k].wait_recv()
            far_more[k].wait_recv()
            left = (
                kept[k, here, :part]
                + far_in[k, here, :].astype(F32)
                + pair_more_in[k].astype(F32)
            )
            right = (
                kept[k, here, part:] + pair_in[k, 1].astype(F32) + far_more_in[k].astype(F32)
            )
            if k == 0:
                half[:, :part] = left
                half[:, part:] = right
            else:
                down_out[k - 1, :, :part] = left.astype(BF16)
                down_out[k - 1, :, part:] = right.astype(BF16)
                to_down.append(
                    go(
                        Send(
                            down_out.at[k - 1],
                            down_in.at[k - 1],
                            red_sems,
                            first_down + k - 1,
                            column[k - 1],
                        )
                    )
                )
    page_copy.wait_recv()
    for i in range(pages.shape[0]):
        page = pl.ds(i * page_rows, page_rows)
        for side, source in ((x, page_out.at[x]), (1 - x, page_in)):
            kv_pages[i, :, half_cols(side)] = source[page, :part]
            kv_pages[i, :, half_cols(2 + side)] = source[page, part:]
    for copy in to_down:
        copy.wait_recv()
    amount = half[...]
    for k in range(groups - 1):
        amount += down_in[k].astype(F32)
    out[...] = amount
    for copy in sent + swaps:
        copy.wait_send()


def whole_layer(
    query,
    key,
    value,
    segments,
    pads,
    choices,
    pages,
    shared_gate,
    shared_up,
    shared_down,
    out_weight,
    residual,
    gain,
    router,
    shared_vector,
    gate,
    up,
    down,
):
    seq_count = lax.axis_size("seq")
    groups = seq_count // 2
    tokens, width = query.shape
    depth, all_units = shared_gate.shape
    units = all_units // seq_count
    total, features = seq_count * tokens, 4 * width
    count = 2 * groups - 1
    hops = 2 * (groups - 1)
    per_token, page_count = choices.shape[0], pages.shape[0]

    def vmem(*shape, dtype=BF16):
        return pltpu.VMEM(shape, dtype)

    def sems(number):
        return [pltpu.SemaphoreType.DMA((number,))] * 2

    block = jax.ShapeDtypeStruct((tokens, width), F32)
    return pl.pallas_call(
        functools.partial(layer_kernel, seq_count, per_token),
        out_shape=(
            block,
            block,
            jax.ShapeDtypeStruct((page_count, tokens // page_count, 2 * width), BF16),
        ),
        in_specs=[pl.BlockSpec(memory_space=pl.ANY)] * 18,
        out_specs=[pl.BlockSpec(memory_space=pltpu.VMEM)] * 3,
        scratch_shapes=[
            vmem(seq_count, 8, tokens, dtype=jnp.int32),
            vmem(tokens, dtype=jnp.int32),
            vmem(tokens, dtype=jnp.int32),
            vmem(per_token, tokens, dtype=jnp.int32),
            pltpu.SMEM((page_count,), jnp.int32),
            vmem(2, tokens, width // 2),
            vmem(total, width),
            vmem(depth, all_units),
            vmem(depth, all_units),
            vmem(all_units, depth),
            vmem(all_units, depth),
            vmem(units, features),
            vmem(units, features),
            vmem(units, features),
            vmem(*out_weight.shape),
            vmem(tokens, width),
            vmem(width),
            vmem(*router.shape),
            vmem(*shared_vector.shape),
            vmem(2 * seq_count, features),
            vmem(*gate.shape),
            vmem(*up.shape),
            vmem(*down.shape),
            vmem(2 * tokens, total, dtype=F32),
            vmem(2, tokens, width // 2),
            vmem(tokens, width),
            vmem(2, tokens, width),
            vmem(tokens, width),
            vmem(3, tokens, width),
            vmem(3, tokens, width),
            vmem(2, 8, tokens, dtype=F32),
            vmem(3, 8, tokens, dtype=F32),
            vmem(seq_count, 8, tokens, dtype=F32),
            vmem(tokens, width),
            vmem(total, features),
            vmem(total, gate.shape[0]),
            vmem(total, units),
            vmem(groups, 2, 2 * tokens, width),
            vmem(groups, 2, 2 * tokens, width),
            vmem(groups, 2 * tokens, width // 2),
            vmem(groups, 2 * tokens, width // 2),
            vmem(groups, 2, tokens, width // 2),
            vmem(groups, 2, tokens, width // 2),
            vmem(groups, tokens, width // 2),
            vmem(groups, tokens, width // 2),
            vmem(groups, tokens, width // 2),
            vmem(groups, tokens, width // 2),
            vmem(groups - 1, tokens, width),
            vmem(groups - 1, tokens, width),
            vmem(groups, 2 * tokens, width, dtype=F32),
            vmem(groups, 2 * tokens, width, dtype=F32),
            vmem(tokens, width, dtype=F32),
            pltpu.SemaphoreType.DMA((24,)),
        ]
        + sems(2 * hops + 5)
        + sems(seq_count - 1)
        + sems(3 * (seq_count - 1))
        + sems(6 + seq_count - 1)
        + sems(hops + 7 * count)
        + sems(7 * groups - 1),
        compiler_params=pltpu.CompilerParams(
            collective_id=0, has_side_effects=True, vmem_limit_bytes=56 * 2**20
        ),
        cost_estimate=pl.CostEstimate(
            flops=8_000_000_000, transcendentals=1_000_000, bytes_accessed=30_000_000
        ),
    )(
        query,
        key,
        value,
        segments,
        pads,
        choices,
        pages,
        shared_gate,
        shared_up,
        shared_down,
        out_weight,
        residual,
        gain,
        router,
        shared_vector,
        gate,
        up,
        down,
    )


def head_scores(query_heads, key_heads):
    score_scale = query_heads.shape[-1] ** (-0.5)
    return (
        jnp.einsum("qhd,khd->hqk", query_heads, key_heads, preferred_element_type=jnp.float32)
        * score_scale
    )


def run_experts(rows_in, gate_weight, up_weight, down_weight):
    local_experts = gate_weight.shape[0]
    sources = rows_in.shape[0] // local_experts
    grouped = rows_in.reshape(sources, local_experts, rows_in.shape[1], rows_in.shape[2])
    gate_act = jnp.einsum(
        "nesd,edf->nesf", grouped, gate_weight, preferred_element_type=jnp.float32
    )
    up_act = jnp.einsum("nesd,edf->nesf", grouped, up_weight, preferred_element_type=jnp.float32)
    hidden = (jax.nn.silu(gate_act) * up_act).astype(jnp.bfloat16)
    partial_out = jnp.einsum(
        "nesf,efd->nesd", hidden, down_weight, preferred_element_type=jnp.float32
    )
    partial_out = partial_out.reshape(rows_in.shape[0], rows_in.shape[1], down_weight.shape[2])
    summed = lax.psum_scatter(
        partial_out.astype(jnp.bfloat16), "tp", scatter_dimension=2, tiled=True
    )
    return lax.all_to_all(summed, "seq", split_axis=0, concat_axis=0, tiled=True)


def per_device(
    query_rows,
    key_rows,
    value_rows,
    residual,
    out_weight,
    norm_gain,
    router_weight,
    expert_ids,
    gate_weight,
    up_weight,
    down_weight,
    shared_gate_weight,
    shared_up_weight,
    shared_down_weight,
    shared_gate_vector,
    segment_ids,
    pad_mask,
    page_table,
):
    tokens_here = query_rows.shape[0]
    feat_width = query_rows.shape[1]
    heads_here = feat_width // HD
    seq_count = lax.axis_size("seq")
    me = lax.axis_index("seq")
    expert_count = seq_count * gate_weight.shape[0]
    per_token = expert_ids.shape[1]
    pages_here = page_table.shape[0]
    page_rows = tokens_here // pages_here
    capacity = 2 * tokens_here * per_token // expert_count
    query_heads = query_rows.reshape(tokens_here, heads_here, HD)
    dense = (
        capacity >= tokens_here
        and gate_weight.shape[0] == 1
        and seq_count % 2 == 0
        and lax.axis_size("tp") == 4
        and per_token <= 5
        and seq_count == 8
    )
    if dense:
        stream, mixture, kv_cache = whole_layer(
            query_rows,
            key_rows,
            value_rows,
            segment_ids,
            pad_mask,
            expert_ids.T,
            page_table,
            shared_gate_weight,
            shared_up_weight,
            shared_down_weight,
            out_weight,
            residual,
            norm_gain,
            router_weight.T,
            shared_gate_vector,
            gate_weight[0].T,
            up_weight[0].T,
            down_weight[0],
        )
        return stream + mixture, kv_cache
    kv_local = jnp.concatenate([key_rows, value_rows], 1)
    notes = jnp.concatenate([segment_ids, pad_mask, expert_ids.T.reshape(-1), page_table])
    all_notes = lax.all_gather(notes, "seq", axis=0, tiled=False)
    gathered_kv = lax.all_gather(kv_local, "seq", axis=0, tiled=True)
    window = min(seq_count, REACH + 1)
    first = jnp.clip(me - REACH, 0, seq_count - window)
    if window == seq_count:
        all_kv, window_notes = gathered_kv, all_notes
    else:
        all_kv = lax.dynamic_slice_in_dim(gathered_kv, first * tokens_here, window * tokens_here, 0)
        window_notes = lax.dynamic_slice_in_dim(all_notes, first, window, 0)
    key_segment = window_notes[:, :tokens_here].reshape(-1)
    key_mask = window_notes[:, tokens_here : 2 * tokens_here].reshape(-1)
    query_place = (me - first) * tokens_here + jnp.arange(tokens_here, dtype=jnp.int32)
    key_place = jnp.arange(window * tokens_here, dtype=jnp.int32)
    all_visible = (
        (segment_ids[:, None] == key_segment[None, :])
        & (key_place[None, :] <= query_place[:, None])
        & ((key_mask[None, :] == 1) | (key_place[None, :] == query_place[:, None]))
    )
    key_heads = all_kv[:, :feat_width].reshape(-1, heads_here, HD)
    scores = jnp.where(all_visible[None], head_scores(query_heads, key_heads), -jnp.inf)
    row_top = jnp.max(scores, -1)
    weights_raw = jnp.exp(scores - row_top[..., None])
    row_total = jnp.sum(weights_raw, -1)
    all_values = all_kv[:, feat_width:].reshape(-1, heads_here, HD)
    mixed_heads = jnp.einsum(
        "hqk,khd->qhd",
        weights_raw.astype(jnp.bfloat16),
        all_values,
        preferred_element_type=jnp.float32,
    )
    all_slots = all_notes[:, -pages_here:].reshape(-1)
    my_slots = me * pages_here + jnp.arange(pages_here, dtype=jnp.int32)
    my_pages = jnp.argmax(all_slots[None, :] == my_slots[:, None], 1)
    kv_cache = jnp.stack(
        [
            lax.dynamic_slice_in_dim(gathered_kv, my_pages[page] * page_rows, page_rows, 0)
            for page in range(pages_here)
        ]
    )
    attended = (
        (mixed_heads / row_total.T[:, :, None])
        .astype(jnp.bfloat16)
        .reshape(tokens_here, feat_width)
    )
    projected = jnp.dot(attended, out_weight, preferred_element_type=jnp.float32)
    projected = lax.psum_scatter(
        projected.astype(jnp.bfloat16), "tp", scatter_dimension=1, tiled=True
    ).astype(jnp.float32)
    stream = residual.astype(jnp.float32) + projected
    square_sum = lax.psum(jnp.sum(stream * stream, 1), "tp")
    normed = (
        stream * lax.rsqrt(square_sum / D + norm_eps)[:, None] * norm_gain.astype(jnp.float32)
    ).astype(jnp.bfloat16)
    full_normed = lax.all_gather(normed, "tp", axis=1, tiled=True)
    logits = jnp.dot(full_normed, router_weight, preferred_element_type=jnp.float32)
    shared_gate_act = jnp.dot(
        full_normed,
        lax.all_gather(shared_gate_weight, "seq", axis=0, tiled=True),
        preferred_element_type=jnp.float32,
    )
    shared_up_act = jnp.dot(
        full_normed,
        lax.all_gather(shared_up_weight, "seq", axis=0, tiled=True),
        preferred_element_type=jnp.float32,
    )
    shared_hidden = (jax.nn.silu(shared_gate_act) * shared_up_act).astype(jnp.bfloat16)
    shared_part = jnp.dot(
        shared_hidden,
        lax.all_gather(shared_down_weight, "seq", axis=1, tiled=True),
        preferred_element_type=jnp.float32,
    )
    shared_out = lax.psum_scatter(
        shared_part.astype(jnp.bfloat16), "tp", scatter_dimension=1, tiled=True
    ).astype(jnp.float32)
    shared_scale = jax.nn.sigmoid(
        jnp.dot(full_normed, shared_gate_vector, preferred_element_type=jnp.float32)
    )
    flat_expert = expert_ids.reshape(-1)
    expert_range = jnp.arange(expert_count, dtype=jnp.int32)
    onehot = (flat_expert[:, None] == expert_range[None, :]).astype(BF16)
    place_range = jnp.arange(flat_expert.shape[0], dtype=jnp.int32)
    earlier = (place_range[:, None] >= place_range[None, :]).astype(BF16)
    running = jnp.dot(earlier, onehot, preferred_element_type=F32)
    slot_rank = jnp.sum(running * onehot.astype(F32), 1).astype(jnp.int32) - 1
    slot_index = flat_expert * capacity + slot_rank
    token_of = jnp.arange(tokens_here * per_token, dtype=jnp.int32) // per_token
    source_row = (
        jnp.full((expert_count * capacity,), tokens_here, jnp.int32).at[slot_index].set(token_of)
    )
    slice_width = normed.shape[1]
    padded_rows = jnp.concatenate([normed, jnp.zeros((1, slice_width), jnp.bfloat16)], 0)
    outgoing = padded_rows[source_row].reshape(expert_count, capacity, slice_width)
    whole_rows = lax.all_gather(
        lax.all_to_all(outgoing, "seq", split_axis=0, concat_axis=0, tiled=True),
        "tp",
        axis=2,
        tiled=True,
    )
    returned = run_experts(whole_rows, gate_weight, up_weight, down_weight)
    chosen = expert_ids[:, :, None] == expert_range[None, None, :]
    chosen_logits = jnp.sum(jnp.where(chosen, logits[:, None, :], 0.0), 2)
    choice_top = jnp.max(chosen_logits, 1, keepdims=True)
    choice_exp = jnp.exp(chosen_logits - choice_top)
    route_weight = choice_exp / jnp.sum(choice_exp, 1, keepdims=True)
    back_rows = returned.reshape(expert_count * capacity, returned.shape[2])[slot_index]
    weighted = (
        back_rows.astype(jnp.float32).reshape(tokens_here, per_token, returned.shape[2])
        * route_weight[:, :, None]
    )
    layer_out = stream + jnp.sum(weighted, 1) + shared_scale[:, None] * shared_out
    return (layer_out, kv_cache)


def solution(mesh):
    placed = (
        P("seq", "tp"),
        P("seq", "tp"),
        P("seq", "tp"),
        P("seq", "tp"),
        P("tp", None),
        P("tp"),
        P(),
        P("seq", None),
        P("seq", None, "tp"),
        P("seq", None, "tp"),
        P("seq", "tp", None),
        P("seq", "tp"),
        P("seq", "tp"),
        P("tp", "seq"),
        P(),
        P("seq"),
        P("seq"),
        P("seq"),
    )
    return jax.shard_map(
        per_device,
        mesh=mesh,
        in_specs=placed,
        out_specs=(P("seq", "tp"), P("seq", None, "tp")),
        check_vma=False,
    )
```
